256 devices in a mesh: blk: 32 (over z, x), grp: 8 (over y, core).
Axes of the slice: x: 4, y: 4, z: 8, core: 2. Of those that a mesh axis runs over, the one named last changes fastest.
Arguments:
- queries: bfloat16 [131072, 512], P(('blk', 'grp')), may hold values from -64 to 64
- keys: bfloat16 [131072, 128], P(('blk', 'grp')), may hold values from -8 to 8
- values: bfloat16 [131072, 128], P(('blk', 'grp')), may hold values from -6 to 6
- selected: int32 [256, 16], replicated, may hold values from 0 to 2047, as said below
- key_in: bfloat16 [4096, 256], replicated, may hold values from -0.09375 to 0.09375
- key_out: bfloat16 [256, 128], replicated, may hold values from -0.375 to 0.375
- value_in: bfloat16 [4096, 256], replicated, may hold values from -0.09375 to 0.09375
- value_out: bfloat16 [256, 128], replicated, may hold values from -0.375 to 0.375
- positions: bfloat16 [2, 32, 128], replicated, may hold values from -5 to 5
- gate_weight: bfloat16 [512, 12], replicated, may hold values from -0.25 to 0.25
Outputs:
- attended: bfloat16 [131072, 512], P(('blk', 'grp'))
The draws below stay inside these ranges and needn't reach their ends.
Inputs may be any that keep to these rules, and one draw needn't show every extreme that they name: `selected`: row d lists 16 different fine blocks. Write r = 64 and b = d // 8. Entry 0 is the first fine block of group d's own tokens. Every listed block j with j // r different from b has j // r < b, and no two listed blocks share a value of j // r other than b. Blocks with j // r == b may lie after group d's tokens.
All inputs are finite; a program needn't handle non-finite values.
Results may differ from the reference program's by a relative error of at most 0.004.
Values may be sent and summed in bfloat16 or wider, within the bound.
No kernel may reach another device: no remote copies, remote signals or barrier semaphores. Data moves between devices by JAX's collectives and lax.ppermute only.
A program may use at most 64 MiB of HBM per device.

```python
import jax
import jax.numpy as jnp
from jax import lax

HEAD_DIM = 128
HEADS = 4
CMP_HIDDEN = 256
CMP_BLOCK = 32
SEL_BLOCK = 64
TOPN = 16
WINDOW = 512
TOK_DEV = 512
SEQ = 131072
NCMP = 4096
GROUPS = 256
N_BLK = 32
N_GRP = 8


def keys_law(key):
    base_key = jax.random.fold_in(key, 11)
    second_key = jax.random.fold_in(base_key, 1)
    return jnp.clip(jax.random.normal(second_key, (SEQ, HEAD_DIM), jnp.float32), -6.0, 6.0)


def draw_keys(key, part):
    return keys_law(key).astype(jnp.bfloat16)


def draw_queries(key, part):
    own_key = jax.random.fold_in(key, 5)
    base = jnp.clip(jax.random.normal(own_key, (SEQ, HEADS * HEAD_DIM), jnp.float32), -6.0, 6.0)
    return base.astype(jnp.bfloat16)


def draw_selected(key, part):
    groups = N_BLK * N_GRP
    per_row = N_GRP * TOK_DEV // SEL_BLOCK
    base_key = jax.random.fold_in(key, 23)
    key_rows, key_blocks, key_own = jax.random.split(base_key, 3)
    group_ids = jnp.arange(groups, dtype=jnp.int32)
    group_row = group_ids // N_GRP
    group_col = group_ids % N_GRP
    row_ids = jnp.arange(N_BLK, dtype=jnp.int32)
    row_score = jax.random.randint(key_rows, (groups, N_BLK), 1, 1 << 20) * N_BLK + row_ids[None, :]
    row_score = jnp.where(row_ids[None, :] == 0, 1 << 28, row_score)
    eligible = row_ids[None, :] < group_row[:, None]
    row_score = jnp.where(eligible, row_score, -1)
    rank = jnp.sum((row_score[:, None, :] > row_score[:, :, None]).astype(jnp.int32), axis=2)
    chosen = eligible & (rank < TOPN - 1)
    remote_count = jnp.sum(chosen.astype(jnp.int32), axis=1)
    slots = jnp.arange(TOPN - 1, dtype=jnp.int32)
    hit = chosen[:, None, :] & (rank[:, None, :] == slots[None, :, None])
    row_of_slot = jnp.sum(jnp.where(hit, row_ids[None, None, :], 0), axis=2)
    remote_blocks = row_of_slot * per_row + jax.random.randint(key_blocks, (groups, TOPN - 1), 0, per_row)
    first_local = group_col * (TOK_DEV // SEL_BLOCK)
    local_ids = jnp.arange(per_row, dtype=jnp.int32)
    own_score = jax.random.randint(key_own, (groups, per_row), 0, 1 << 20) * per_row + local_ids[None, :]
    own_score = jnp.where(local_ids[None, :] == first_local[:, None], -1, own_score)
    best_scores, unused = jax.lax.top_k(own_score, TOPN - 1)
    own_extra = group_row[:, None] * per_row + best_scores % per_row
    own_index = jnp.clip(slots[None, :] - remote_count[:, None], 0, TOPN - 2)
    own_pick = jnp.take_along_axis(own_extra, own_index, axis=1)
    tail = jnp.where(slots[None, :] < remote_count[:, None], remote_blocks, own_pick)
    head = (group_row * per_row + first_local)[:, None]
    return jnp.concatenate([head, tail], axis=1).astype(jnp.int32)


def level_of(key, extent, cuts, low, high):
    def one(axis_at, shards_of):
        heights = jax.random.uniform(jax.random.fold_in(jax.random.fold_in(key, 6), axis_at), (shards_of,), jnp.float32, low / len(cuts), high / len(cuts))
        return jnp.repeat(jnp.exp(heights), extent[axis_at] // shards_of).reshape((-1,) + (1,) * (len(extent) - axis_at - 1))

    level = one(*cuts[0])
    for cut in cuts[1:]:
        level = level * one(*cut)
    return level


def centred(rng, shape, deviation, limit, cuts=(), kind=jnp.bfloat16):
    values = jax.random.normal(rng, shape, jnp.float32) * deviation
    if len(cuts) > 0:
        values = level_of(rng, shape, cuts, -0.22, 0.18) * values
    return jnp.clip(values, min=-limit, max=limit).astype(kind)


def setup_inputs(seed: int = 0) -> dict:
    streams_of = jax.random.split(jax.random.key(seed), 11)
    queries = draw_queries(jax.random.fold_in(streams_of[10], 71), 0)
    keys = draw_keys(jax.random.fold_in(streams_of[10], 71), 0)
    values = centred(streams_of[2], (SEQ, HEAD_DIM), 1.0, 6.0, ((0, 256),))
    selected = draw_selected(jax.random.fold_in(streams_of[10], 71), 0)
    key_in = centred(streams_of[4], (CMP_BLOCK * HEAD_DIM, CMP_HIDDEN), (CMP_BLOCK * HEAD_DIM) ** -0.5, 0.09375)
    key_out = centred(streams_of[5], (CMP_HIDDEN, HEAD_DIM), CMP_HIDDEN ** -0.5, 0.375)
    value_in = centred(streams_of[6], (CMP_BLOCK * HEAD_DIM, CMP_HIDDEN), (CMP_BLOCK * HEAD_DIM) ** -0.5, 0.09375)
    value_out = centred(streams_of[7], (CMP_HIDDEN, HEAD_DIM), CMP_HIDDEN ** -0.5, 0.375)
    positions = centred(streams_of[8], (2, CMP_BLOCK, HEAD_DIM), 1.0, 5.0)
    gate_weight = centred(streams_of[9], (HEADS * HEAD_DIM, 3 * HEADS), (HEADS * HEAD_DIM) ** -0.5, 0.25)
    return dict(queries=queries, keys=keys, values=values, selected=selected, key_in=key_in, key_out=key_out, value_in=value_in, value_out=value_out, positions=positions, gate_weight=gate_weight)


NEG = -1e30


def compress(tokens, shift, w_in, w_out):
    count = tokens.shape[0] // CMP_BLOCK
    mixed = tokens.astype(jnp.float32).reshape(count, CMP_BLOCK, HEAD_DIM) + shift.astype(jnp.float32)[None]
    flat = mixed.astype(jnp.bfloat16).reshape(count, CMP_BLOCK * HEAD_DIM)
    hidden = jax.nn.silu(jnp.dot(flat, w_in, preferred_element_type=jnp.float32)).astype(jnp.bfloat16)
    return jnp.dot(hidden, w_out, preferred_element_type=jnp.float32).astype(jnp.bfloat16)


def attend(query_rows, query_pos, key_rows, value_rows, key_pos, span):
    scale = HEAD_DIM ** -0.5
    scores = jnp.einsum("qhd,kd->qhk", query_rows.astype(jnp.float32), key_rows.astype(jnp.float32)) * scale
    allowed = (key_pos[None, :] <= query_pos[:, None]) & (key_pos[None, :] > query_pos[:, None] - span) & (key_pos[None, :] >= 0)
    scores = jnp.where(allowed[:, None, :], scores, NEG)
    top = jnp.max(scores, axis=2, keepdims=True)
    weights = jnp.exp(scores - top)
    total = jnp.sum(weights, axis=2)
    mixed = jnp.einsum("qhk,kd->qhd", weights.astype(jnp.bfloat16).astype(jnp.float32), value_rows.astype(jnp.float32))
    return mixed / total[..., None]


def reference(queries, keys, values, selected, key_in, key_out, value_in, value_out, positions, gate_weight):
    scale = HEAD_DIM ** -0.5
    comp_keys = compress(keys, positions[0], key_in, key_out)
    comp_values = compress(values, positions[1], value_in, value_out)
    comp_end = jnp.arange(NCMP, dtype=jnp.int32) * CMP_BLOCK + (CMP_BLOCK - 1)
    padded_keys = jnp.concatenate([jnp.zeros((WINDOW, HEAD_DIM), keys.dtype), keys], axis=0)
    padded_values = jnp.concatenate([jnp.zeros((WINDOW, HEAD_DIM), values.dtype), values], axis=0)

    def group(index):
        first = index * TOK_DEV
        flat_rows = lax.dynamic_slice_in_dim(queries, first, TOK_DEV, 0)
        rows = flat_rows.reshape(TOK_DEV, HEADS, HEAD_DIM)
        query_pos = first + jnp.arange(TOK_DEV, dtype=jnp.int32)
        scores = jnp.einsum("qhd,kd->qhk", rows.astype(jnp.float32), comp_keys.astype(jnp.float32)) * scale
        seen = comp_end[None, :] <= query_pos[:, None]
        scores = jnp.where(seen[:, None, :], scores, NEG)
        top = jnp.maximum(jnp.max(scores, axis=2, keepdims=True), 0.0)
        weights = jnp.exp(scores - top)
        total = jnp.exp(-top[..., 0]) + jnp.sum(weights, axis=2)
        coarse = jnp.einsum("qhk,kd->qhd", weights.astype(jnp.bfloat16).astype(jnp.float32), comp_values.astype(jnp.float32)) / total[..., None]
        chosen = lax.dynamic_index_in_dim(selected, index, 0, keepdims=False)
        token_ids = (chosen[:, None] * SEL_BLOCK + jnp.arange(SEL_BLOCK, dtype=jnp.int32)[None, :]).reshape(-1)
        fine = attend(rows, query_pos, jnp.take(keys, token_ids, axis=0), jnp.take(values, token_ids, axis=0), token_ids, SEQ + 1)
        window_keys = lax.dynamic_slice_in_dim(padded_keys, first, TOK_DEV + WINDOW, 0)
        window_values = lax.dynamic_slice_in_dim(padded_values, first, TOK_DEV + WINDOW, 0)
        window_pos = first - WINDOW + jnp.arange(TOK_DEV + WINDOW, dtype=jnp.int32)
        local = attend(rows, query_pos, window_keys, window_values, window_pos, WINDOW)
        gates = jax.nn.sigmoid(jnp.dot(flat_rows, gate_weight, preferred_element_type=jnp.float32)).reshape(TOK_DEV, 3, HEADS)
        mixed = gates[:, 0, :, None] * coarse + gates[:, 1, :, None] * fine + gates[:, 2, :, None] * local
        return mixed.astype(jnp.bfloat16).reshape(TOK_DEV, HEADS * HEAD_DIM)

    result = lax.map(group, jnp.arange(GROUPS, dtype=jnp.int32))
    return result.reshape(SEQ, HEADS * HEAD_DIM)
```

```python
import math

import jax
import jax.numpy as jnp
from jax import lax
from jax.experimental import pallas as pl
from jax.experimental.pallas import tpu as pltpu
from jax.sharding import PartitionSpec as P

HEAD_DIM = 128
HEADS = 4
CMP_BLOCK = 32
SEL_BLOCK = 64
TOPN = 16
WINDOW = 512
NEG = -1e30
SCALE2 = HEAD_DIM**-0.5 * math.log2(math.e)
AXES = ("blk", "grp")
ANY = pl.BlockSpec(memory_space=pl.ANY)
SMEM = pl.BlockSpec(memory_space=pltpu.SMEM)
VMEM = pl.BlockSpec(memory_space=pltpu.VMEM)


def compress(tokens, shift, w_in, w_out):
    count = tokens.shape[0] // CMP_BLOCK
    mixed = (
        tokens.astype(jnp.float32).reshape(count, CMP_BLOCK, HEAD_DIM)
        + shift.astype(jnp.float32)[None]
    )
    flat = mixed.astype(jnp.bfloat16).reshape(count, CMP_BLOCK * HEAD_DIM)
    hidden = jax.nn.silu(jnp.dot(flat, w_in, preferred_element_type=jnp.float32)).astype(
        jnp.bfloat16
    )
    return jnp.dot(hidden, w_out, preferred_element_type=jnp.float32).astype(jnp.bfloat16)


def route(stretches, rows, cores, move):
    pairs = []
    for b in range(stretches):
        for y in range(rows):
            for c in range(cores):
                to_y, to_c = move(y, c)
                pairs.append(((b * rows + y) * cores + c, (b * rows + to_y % rows) * cores + to_c))
    return pairs


def dot_t(a, b):
    return lax.dot_general(a, b, (((1,), (1,)), ((), ())), preferred_element_type=jnp.float32)


def lane_groups(x, op):
    parts = [x[:, i : i + 128] for i in range(0, x.shape[1], 128)]
    while len(parts) > 1:
        parts = [
            op(parts[i], parts[i + 1]) if i + 1 < len(parts) else parts[i]
            for i in range(0, len(parts), 2)
        ]
    return parts[0]


def gates_of(q, gw):
    return jax.nn.sigmoid(jnp.dot(q, gw, preferred_element_type=jnp.float32))


def copy_all(pairs, sem):
    copies = [pltpu.make_async_copy(s, d, sem.at[i]) for i, (s, d) in enumerate(pairs)]
    for c in copies:
        c.start()
    for c in copies:
        c.wait()


def pick_kernel(picked, near, *refs):
    own, from1, from3, far_a, far_b, s_own, s_from1, s_from3, s_far_a, s_far_b = refs[:10]
    out, nearby, rows, sem = refs[10:]
    half = far_a.shape[0]
    pairs = []
    for dc, (o, a, b, fa, fb) in enumerate(
        ((own, from1, from3, far_a, far_b), (s_own, s_from1, s_from3, s_far_a, s_far_b))
    ):
        for dy, ref in ((0, o), (1, a), (3, b)):
            slot = dy * 2 + dc
            pairs.append((ref, rows.at[pl.ds(slot * 8, 8)]))
        slot = 4 + dc
        pairs.append((fa, rows.at[pl.ds(slot * 8, half)]))
        pairs.append((fb, rows.at[pl.ds(slot * 8 + half, half)]))
    copy_all(pairs, sem)
    for i in range(out.shape[0]):
        out[i] = rows[picked[i]]
    for i in range(nearby.shape[0]):
        nearby[i] = rows[near[i]]


def window_kernel(low, q_ref, prev_ref, kv_ref, gw_ref, out_ref):
    toks = q_ref.shape[0]
    q = q_ref[...]
    gates = gates_of(q, gw_ref[...])
    rows = 128
    for first in range(0, toks, rows):
        k = jnp.concatenate([prev_ref[first:, :HEAD_DIM], kv_ref[: first + rows, :HEAD_DIM]], 0)
        v = jnp.concatenate([prev_ref[first:, HEAD_DIM:], kv_ref[: first + rows, HEAD_DIM:]], 0)
        shape = (rows, WINDOW + rows)
        r = lax.broadcasted_iota(jnp.int32, shape, 0)
        c = lax.broadcasted_iota(jnp.int32, shape, 1)
        seen = (c > r) & (c <= r + WINDOW) & (c + first >= low[0])
        for h in range(HEADS):
            qh = q_ref[first : first + rows, h * HEAD_DIM : (h + 1) * HEAD_DIM]
            s = jnp.where(seen, dot_t(qh, k), NEG)
            top = jnp.max(lane_groups(s, jnp.maximum), axis=1, keepdims=True)
            p = jnp.exp2((s - top) * SCALE2)
            total = jnp.sum(lane_groups(p, jnp.add), axis=1, keepdims=True)
            o = jnp.dot(p.astype(jnp.bfloat16), v, preferred_element_type=jnp.float32)
            g = gates[first : first + rows, 2 * HEADS + h : 2 * HEADS + h + 1]
            out_ref[first : first + rows, h * HEAD_DIM : (h + 1) * HEAD_DIM] = o * (g / total)


def coarse_kernel(last, q_ref, gw_ref, part_ref, ends_ref, *refs):
    own, from1, from3, far_a, far_b, s_own, s_from1, s_from3, s_far_a, s_far_b = refs[:10]
    out_ref, kv, s_buf, mx, ls, acc, sem = refs[10:]
    toks = q_ref.shape[0]
    half = far_a.shape[0]
    pairs = []
    for dc, (o, a, b, fa, fb) in enumerate(
        ((own, from1, from3, far_a, far_b), (s_own, s_from1, s_from3, s_far_a, s_far_b))
    ):
        for dy, ref in ((0, o), (1, a), (3, b)):
            pairs.append((ref, kv.at[:, dy * 2 + dc]))
        pairs.append((fa, kv.at[pl.ds(0, half), 4 + dc]))
        pairs.append((fb, kv.at[pl.ds(half, half), 4 + dc]))
    copy_all(pairs, sem)
    zi = last[0]
    base = last[1]
    gates = gates_of(q_ref[...], gw_ref[...])
    chunk = kv.shape[1] * kv.shape[2]
    seen = ends_ref[pl.ds(zi, 1), :] <= base + lax.broadcasted_iota(jnp.int32, (toks, chunk), 0)

    def rows_of(z):
        return kv[z].reshape(chunk, 2 * HEAD_DIM)

    for h in range(HEADS):
        cols = slice(h * HEAD_DIM, (h + 1) * HEAD_DIM)
        qh = q_ref[:, cols]
        mx[...] = jnp.zeros_like(mx)
        ls[...] = jnp.zeros_like(ls)
        acc[...] = jnp.zeros_like(acc)

        def first(z, _):
            s = dot_t(qh, rows_of(z)[:, :HEAD_DIM])
            s_buf[z] = s
            mx[...] = jnp.maximum(mx[...], lane_groups(s, jnp.maximum))
            return 0

        lax.fori_loop(0, zi, first, 0)
        s = jnp.where(seen, dot_t(qh, rows_of(zi)[:, :HEAD_DIM]), NEG)
        s_buf[zi] = s
        top = jnp.max(jnp.maximum(mx[...], lane_groups(s, jnp.maximum)), axis=1, keepdims=True)

        def second(z, _):
            p = jnp.exp2((s_buf[z] - top) * SCALE2)
            ls[...] += lane_groups(p, jnp.add)
            acc[...] += jnp.dot(
                p.astype(jnp.bfloat16), rows_of(z)[:, HEAD_DIM:], preferred_element_type=jnp.float32
            )
            return 0

        lax.fori_loop(0, zi + 1, second, 0)
        total = jnp.exp2(-top * SCALE2) + jnp.sum(ls[...], axis=1, keepdims=True)
        out_ref[:, cols] = part_ref[:, cols] + acc[...] * (gates[:, h : h + 1] / total)


def fine_kernel(owners, near, base, q_ref, gw_ref, part_ref, pos_ref, in_ref, near_ref, out_ref, kv):
    toks = q_ref.shape[0]
    for i in range(TOPN):
        block = jnp.where(near[i] == 1, near_ref[i], in_ref[owners[i]])
        kv[pl.ds(i * SEL_BLOCK, SEL_BLOCK), :] = block
    gates = gates_of(q_ref[...], gw_ref[...])
    rows = 256
    for first in range(0, toks, rows):
        p0 = base[0] + first
        seen = pos_ref[...] <= p0 + lax.broadcasted_iota(jnp.int32, (rows, kv.shape[0]), 0)
        for h in range(HEADS):
            cols = slice(h * HEAD_DIM, (h + 1) * HEAD_DIM)
            s = jnp.where(seen, dot_t(q_ref[first : first + rows, cols], kv[:, :HEAD_DIM]), NEG)
            top = jnp.max(lane_groups(s, jnp.maximum), axis=1, keepdims=True)
            p = jnp.exp2((s - top) * SCALE2)
            total = jnp.sum(lane_groups(p, jnp.add), axis=1, keepdims=True)
            o = jnp.dot(p.astype(jnp.bfloat16), kv[:, HEAD_DIM:], preferred_element_type=jnp.float32)
            g = gates[first : first + rows, HEADS + h : HEADS + h + 1]
            out = part_ref[first : first + rows, cols] + o * (g / total)
            out_ref[first : first + rows, cols] = out.astype(out_ref.dtype)


def params(mib):
    return pltpu.CompilerParams(vmem_limit_bytes=mib << 20)


def solution(mesh):
    stretches = mesh.shape["blk"]
    group_size = mesh.shape["grp"]
    cores = 2
    ys = group_size // cores
    depth = 8
    up = route(stretches, ys, cores, lambda y, c: (y + 1, c))
    down = route(stretches, ys, cores, lambda y, c: (y - 1, c))
    swap = route(stretches, ys, cores, lambda y, c: (y, 1 - c))
    behind = [(i - 1, i) for i in range(1, stretches * group_size)]

    def spread(piece):
        half = piece.shape[0] // 2
        from1 = lax.ppermute(piece, AXES, up)
        from3 = lax.ppermute(piece, AXES, down)
        far_a = lax.ppermute(from1[:half], AXES, up)
        far_b = lax.ppermute(from3[half:], AXES, down)
        mine = (piece, from1, from3, far_a, far_b)
        return mine + tuple(lax.ppermute(p, AXES, swap) for p in mine)

    def per_device(
        queries, keys, values, selected, key_in, key_out, value_in, value_out, positions, gate_weight
    ):
        stretch = lax.axis_index("blk")
        column = lax.axis_index("grp")
        my_y = column // cores
        my_c = column % cores
        toks = queries.shape[0]
        position = stretch * group_size + column
        per_dev = toks // SEL_BLOCK
        per_row = group_size * per_dev

        kv = jnp.concatenate([keys, values], axis=1)
        pieces = spread(kv.reshape(per_dev, SEL_BLOCK, 2 * HEAD_DIM))
        prev = lax.ppermute(kv, AXES, behind)

        packed = jnp.concatenate(
            [
                compress(keys, positions[0], key_in, key_out),
                compress(values, positions[1], value_in, value_out),
            ],
            axis=1,
        )
        ncomp = toks // CMP_BLOCK
        copies = jnp.broadcast_to(packed[None], (stretches, *packed.shape))
        column_comp = lax.all_to_all(copies, "blk", split_axis=0, concat_axis=0, tiled=True)
        per_z = stretches // depth * ncomp
        comp_pieces = spread(column_comp.reshape(depth, per_z, 2 * HEAD_DIM))

        def slot_of(block):
            owner = block // per_dev
            dy = (my_y - owner // cores) % ys
            return (dy * cores + (owner % cores) ^ my_c) * per_dev + block % per_dev

        requests = lax.dynamic_index_in_dim(
            selected.reshape(stretches, group_size, TOPN), column, 1, keepdims=False
        )
        targets = jnp.arange(stretches, dtype=jnp.int32)
        match = (requests // per_row == stretch) & (targets[:, None] != stretch)
        picked = jnp.sum(jnp.where(match, requests % per_row, 0), axis=1)
        mine = lax.dynamic_index_in_dim(selected, position, 0, keepdims=False)
        owners = mine // per_row

        outgoing, nearby = pl.pallas_call(
            pick_kernel,
            in_specs=[SMEM, SMEM] + [ANY] * 10,
            out_specs=[VMEM, VMEM],
            out_shape=[
                jax.ShapeDtypeStruct((stretches, SEL_BLOCK, 2 * HEAD_DIM), jnp.bfloat16),
                jax.ShapeDtypeStruct((TOPN, SEL_BLOCK, 2 * HEAD_DIM), jnp.bfloat16),
            ],
            scratch_shapes=[
                pltpu.VMEM((per_row, SEL_BLOCK, 2 * HEAD_DIM), jnp.bfloat16),
                pltpu.SemaphoreType.DMA((10,)),
            ],
            compiler_params=params(16),
            name="pick",
        )(slot_of(picked), slot_of(mine % per_row), *pieces)
        incoming = lax.all_to_all(outgoing, "blk", split_axis=0, concat_axis=0, tiled=True)

        f32_rows = jax.ShapeDtypeStruct(queries.shape, jnp.float32)
        low = jnp.where(position == 0, toks, 0).astype(jnp.int32).reshape(1)
        local = pl.pallas_call(
            window_kernel,
            in_specs=[SMEM] + [VMEM] * 4,
            out_specs=VMEM,
            out_shape=f32_rows,
            compiler_params=params(24),
            name="window",
        )(low, queries, prev, kv, gate_weight)

        slots = jnp.arange(ys * cores, dtype=jnp.int32)
        column_of = ((my_y - slots // cores) % ys) * cores + ((slots % cores) ^ my_c)
        blks = jnp.arange(stretches, dtype=jnp.int32).reshape(depth, 1, stretches // depth, 1)
        ends = (
            (blks * group_size + column_of[None, :, None, None]) * ncomp
            + jnp.arange(ncomp, dtype=jnp.int32)[None, None, None, :]
        ) * CMP_BLOCK + (CMP_BLOCK - 1)
        ends = ends.reshape(depth, -1)
        base = (position * toks).astype(jnp.int32)
        last = jnp.stack([stretch // (stretches // depth), base]).astype(jnp.int32)
        chunk = ends.shape[1]
        part = pl.pallas_call(
            coarse_kernel,
            in_specs=[SMEM] + [VMEM] * 4 + [ANY] * 10,
            out_specs=VMEM,
            out_shape=f32_rows,
            scratch_shapes=[
                pltpu.VMEM((depth, ys * cores, per_z, 2 * HEAD_DIM), jnp.bfloat16),
                pltpu.VMEM((depth, toks, chunk), jnp.float32),
                pltpu.VMEM((toks, 128), jnp.float32),
                pltpu.VMEM((toks, 128), jnp.float32),
                pltpu.VMEM((toks, 128), jnp.float32),
                pltpu.SemaphoreType.DMA((10,)),
            ],
            compiler_params=params(40),
            name="coarse",
        )(last, queries, gate_weight, local, ends, *comp_pieces)

        fine_pos = (
            mine[:, None] * SEL_BLOCK + jnp.arange(SEL_BLOCK, dtype=jnp.int32)[None, :]
        ).reshape(1, -1)
        return pl.pallas_call(
            fine_kernel,
            in_specs=[SMEM] * 3 + [VMEM] * 6,
            out_specs=VMEM,
            out_shape=jax.ShapeDtypeStruct(queries.shape, jnp.bfloat16),
            scratch_shapes=[pltpu.VMEM((TOPN * SEL_BLOCK, 2 * HEAD_DIM), jnp.bfloat16)],
            compiler_params=params(40),
            name="fine",
        )(
            owners,
            (owners == stretch).astype(jnp.int32),
            base.reshape(1),
            queries,
            gate_weight,
            part,
            fine_pos,
            incoming,
            nearby,
        )

    rows = P(AXES, None)
    return jax.shard_map(
        per_device,
        mesh=mesh,
        in_specs=(rows, rows, rows) + (P(),) * 7,
        out_specs=rows,
        check_vma=False,
    )
```

```python
import math

import jax
import jax.numpy as jnp
from jax import lax
from jax.experimental import pallas as pl
from jax.experimental.pallas import tpu as pltpu
from jax.sharding import PartitionSpec as P

HEAD_DIM = 128
HEADS = 4
CMP_BLOCK = 32
SEL_BLOCK = 64
TOPN = 16
WINDOW = 512
NEG = -1e30
SCALE2 = HEAD_DIM**-0.5 * math.log2(math.e)
AXES = ("blk", "grp")
ANY = pl.BlockSpec(memory_space=pl.ANY)
HBM = pl.BlockSpec(memory_space=pltpu.MemorySpace.HBM)
SMEM = pl.BlockSpec(memory_space=pltpu.SMEM)
VMEM = pl.BlockSpec(memory_space=pltpu.VMEM)


def route(stretches, rows, cores, move):
    pairs = []
    for b in range(stretches):
        for y in range(rows):
            for c in range(cores):
                to_y, to_c = move(y, c)
                pairs.append(((b * rows + y) * cores + c, (b * rows + to_y % rows) * cores + to_c))
    return pairs


def dot_t(a, b):
    return lax.dot_general(a, b, (((1,), (1,)), ((), ())), preferred_element_type=jnp.float32)


def lane_groups(x, op):
    parts = [x[:, i : i + 128] for i in range(0, x.shape[1], 128)]
    while len(parts) > 1:
        parts = [
            op(parts[i], parts[i + 1]) if i + 1 < len(parts) else parts[i]
            for i in range(0, len(parts), 2)
        ]
    return parts[0]


def gates_of(q_ref, gw_ref):
    return jax.nn.sigmoid(dot_t(q_ref[...], gw_ref[...]))


def start_all(pairs, sem):
    copies = [pltpu.make_async_copy(s, d, sem.at[i]) for i, (s, d) in enumerate(pairs)]
    for copy in copies:
        copy.start()
    return copies


def copy_all(pairs, sem):
    for copy in start_all(pairs, sem):
        copy.wait()


def prep_kernel(ids, keys_ref, values_ref, sel_ref, kv_ref, meta_ref, raw, sel_buf, sem):
    copy_all([(keys_ref, raw.at[0]), (values_ref, raw.at[1]), (sel_ref, sel_buf)], sem)
    kv_ref[:, :HEAD_DIM] = raw[0]
    kv_ref[:, HEAD_DIM:] = raw[1]
    sel = sel_buf[...]
    groups = sel.shape[1]
    group = lax.broadcasted_iota(jnp.int32, sel.shape, 1)
    match = ((sel >> 6) == ids[0]) & ((group >> 3) != ids[0])
    slot = slot_of(sel & 63, ids[1])
    meta_ref[:, :groups] = jnp.sum(jnp.where(match, slot, 0), axis=0, keepdims=True)
    mine = jnp.sum(jnp.where(group == ids[0] * 8 + ids[1], sel, 0), axis=1, keepdims=True)
    lane = lax.broadcasted_iota(jnp.int32, (TOPN, 128), 1)
    entry = lax.broadcasted_iota(jnp.int32, (TOPN, 128), 0)
    row = jnp.sum(jnp.where(lane == entry, mine, 0), axis=0, keepdims=True)
    row = jnp.where(lane[:1] == TOPN, ids[0], row)
    meta_ref[:, groups:] = jnp.where(lane[:1] == TOPN + 1, ids[1], row)


def unpack(meta):
    return meta[0, 256 + TOPN], meta[0, 257 + TOPN], [meta[0, 256 + i] for i in range(TOPN)]


def slot_of(block, column):
    owner = block >> 3
    dy = ((column >> 1) - (owner >> 1)) & 3
    return (((dy << 1) + ((owner ^ column) & 1)) << 3) + (block & 7)


def compress_kernel(
    keys_ref, values_ref, pos_ref, k_in, k_out, v_in, v_out, out_ref, raw, pos, wide, flat, w1, w2, sem
):
    toks = keys_ref.shape[0]
    count = toks // CMP_BLOCK
    loads = start_all(
        [
            (keys_ref, raw.at[0]),
            (pos_ref, pos),
            (values_ref, raw.at[1]),
            (k_in, w1.at[0]),
            (k_out, w2.at[0]),
            (v_in, w1.at[1]),
            (v_out, w2.at[1]),
        ],
        sem,
    )
    for load in loads[:3]:
        load.wait()
    for side in range(2):
        shift = pos[side].astype(jnp.float32)
        x = raw[side].astype(jnp.float32).reshape(count, CMP_BLOCK, HEAD_DIM) + shift[None]
        wide[side] = x.reshape(toks, HEAD_DIM)
        for t in range(CMP_BLOCK):
            rows = wide[side, pl.ds(t, count, stride=CMP_BLOCK), :]
            flat[side, :, t * HEAD_DIM : (t + 1) * HEAD_DIM] = rows.astype(jnp.bfloat16)
    for side in range(2):
        for load in loads[3 + 2 * side : 5 + 2 * side]:
            load.wait()
        hidden = jnp.dot(flat[side], w1[side], preferred_element_type=jnp.float32)
        hidden = (hidden * jax.nn.sigmoid(hidden)).astype(jnp.bfloat16)
        comp = jnp.dot(hidden, w2[side], preferred_element_type=jnp.float32).astype(jnp.bfloat16)
        cols = slice(side * HEAD_DIM, (side + 1) * HEAD_DIM)
        out_ref[:, :, cols] = jnp.broadcast_to(comp[None], (out_ref.shape[0], count, HEAD_DIM))


def piece_pairs(pieces, near, far):
    pairs = []
    for dc in range(2):
        o, a, b, fa, fb = pieces[dc * 5 : dc * 5 + 5]
        for dy, ref in ((0, o), (1, a), (3, b)):
            pairs.append((ref, near(dy * 2 + dc)))
        half = fa.shape[0]
        pairs.append((fa, far(4 + dc, 0, half)))
        pairs.append((fb, far(4 + dc, half, half)))
    return pairs


def pick_kernel(meta, *refs):
    pieces = refs[:10]
    out, nearby, rows, sem = refs[10:]
    copy_all(
        piece_pairs(
            pieces,
            lambda slot: rows.at[pl.ds(slot * 8, 8)],
            lambda slot, at, n: rows.at[pl.ds(slot * 8 + at, n)],
        ),
        sem,
    )
    stretch, column, mine = unpack(meta)
    pairs = [(rows.at[meta[0, i * 8 + column]], out.at[i]) for i in range(out.shape[0])]
    for i in range(TOPN):
        pairs.append((rows.at[slot_of(mine[i] & 63, column)], nearby.at[i]))
    copy_all(pairs, sem)


def fill_ones(values):
    values[:, HEAD_DIM:] = jnp.ones((values.shape[0], HEAD_DIM), values.dtype)


def attend(q, keys, values, seen):
    s = dot_t(q, keys)
    if seen is not None:
        s = jnp.where(seen, s, NEG)
    top = jnp.max(lane_groups(s, jnp.maximum), axis=1, keepdims=True)
    p = jnp.exp2((s - top) * SCALE2).astype(jnp.bfloat16)
    o = jnp.dot(p, values, preferred_element_type=jnp.float32)
    return o[:, :HEAD_DIM], o[:, HEAD_DIM:]


def window_kernel(
    meta, q_in, gw_in, kv_in, s_own, s_from1, edge, out, q_ref, gw_ref, out_ref, keys, values, sem
):
    loads = start_all([(q_in, q_ref), (gw_in, gw_ref)], sem.at[pl.ds(4, 2)])
    stretch, column, _ = unpack(meta)
    toks = q_in.shape[0]
    heads = slice(0, HEAD_DIM)
    tails = slice(HEAD_DIM, 2 * HEAD_DIM)

    def fetch(ref, at, i):
        copy_all(
            [
                (ref.at[:, heads], keys.at[pl.ds(at, toks)]),
                (ref.at[:, tails], values.at[pl.ds(at, toks), heads]),
            ],
            sem.at[pl.ds(2 * i, 2)],
        )

    @pl.when(column % 2 == 1)
    def _():
        fetch(s_own, 0, 0)

    @pl.when((column % 2 == 0) & (column > 0))
    def _():
        fetch(s_from1, 0, 0)

    @pl.when(column == 0)
    def _():
        fetch(edge, 0, 0)

    fetch(kv_in, toks, 1)
    fill_ones(values)
    for load in loads:
        load.wait()
    low = jnp.where(stretch * 8 + column == 0, toks, 0)
    gates = gates_of(q_ref, gw_ref)
    rows = 128
    for first in range(0, toks, rows):
        span = slice(first, first + WINDOW + rows)
        r = lax.broadcasted_iota(jnp.int32, (rows, WINDOW + rows), 0)
        c = lax.broadcasted_iota(jnp.int32, (rows, WINDOW + rows), 1)
        seen = (c > r) & (c <= r + WINDOW) & (c + first >= low)
        for h in range(HEADS):
            cols = slice(h * HEAD_DIM, (h + 1) * HEAD_DIM)
            o, total = attend(q_ref[first : first + rows, cols], keys[span], values[span], seen)
            g = gates[first : first + rows, 2 * HEADS + h : 2 * HEADS + h + 1]
            out_ref[first : first + rows, cols] = o * (g / total)
    copy_all([(out_ref, out)], sem.at[pl.ds(6, 1)])


NEAR_SLOTS = ((0, 0), (0, 1), (1, 0), (1, 1), (3, 0), (3, 1))
FAR_SLOTS = ((2, 0), (2, 1))


def coarse_ends(stretch_z, zs, slots, column):
    lane = lax.broadcasted_iota(jnp.int32, (1, zs * len(slots) * 64), 1)
    z = jnp.zeros_like(lane)
    for i in range(1, zs):
        z += (lane >= i * len(slots) * 64).astype(jnp.int32)
    place = (lane >> 6) - z * len(slots)
    owner = jnp.zeros_like(lane)
    for i, (dy, dc) in enumerate(slots):
        theirs = ((((column >> 1) - dy) & 3) << 1) + ((column ^ dc) & 1)
        owner = jnp.where(place == i, theirs, owner)
    blk = ((stretch_z + z) << 2) + ((lane >> 4) & 3)
    return (((blk << 3) + owner) * 16 + (lane & 15)) * CMP_BLOCK + (CMP_BLOCK - 1)


def load_coarse(pairs, keys, values, sem):
    copies = []
    for ref, at in pairs:
        copies.append((ref.at[:, :, :HEAD_DIM], keys.at[at]))
        copies.append((ref.at[:, :, HEAD_DIM:], values.at[(*at, slice(None), slice(0, HEAD_DIM))]))
    loads = start_all(copies, sem)
    values[..., HEAD_DIM:] = jnp.ones((*values.shape[:3], HEAD_DIM), values.dtype)
    return loads


def fold(q, keys, values, seen, old):
    s = dot_t(q, keys)
    if seen is not None:
        s = jnp.where(seen, s, NEG)
    acc, total, best = old
    top = jnp.maximum(best, jnp.max(lane_groups(s, jnp.maximum), axis=1, keepdims=True))
    wide = jnp.concatenate([top] * (s.shape[1] // 128), axis=1)
    p = jnp.exp2((s - wide) * SCALE2).astype(jnp.bfloat16)
    factor = jnp.exp2((best - top) * SCALE2)
    o = jnp.dot(p, values, preferred_element_type=jnp.float32)
    return acc * factor + o[:, :HEAD_DIM], total * factor + o[:, HEAD_DIM:], top


ROWS = 256
PARTS = (slice(0, 128), slice(128, 256), slice(256, 384))


def near_kernel(meta, q_in, own, s_own, from1, s_from1, from3, s_from3, state, q_ref, keys, values, sem):
    q_load = pltpu.make_async_copy(q_in, q_ref, sem.at[12])
    q_load.start()
    stretch, column, _ = unpack(meta)
    toks = q_in.shape[0]
    pieces = (own, s_own, from1, s_from1, from3, s_from3)
    loads = load_coarse([(ref, (slice(None), i)) for i, ref in enumerate(pieces)], keys, values, sem)
    state[:, :, PARTS[0]] = jnp.zeros((HEADS, toks, 128), jnp.float32)
    state[:, :, PARTS[1]] = jnp.ones((HEADS, toks, 128), jnp.float32)
    state[:, :, PARTS[2]] = jnp.zeros((HEADS, toks, 128), jnp.float32)
    for load in [q_load, *loads]:
        load.wait()
    pair = stretch >> 3
    chunk = 2 * len(NEAR_SLOTS) * 64
    ends = coarse_ends(pair << 1, 2, NEAR_SLOTS, column)
    base = (stretch * 8 + column) * toks

    def step(z, masked):
        k = keys[pl.ds(2 * z, 2)].reshape(chunk, HEAD_DIM)
        v = values[pl.ds(2 * z, 2)].reshape(chunk, 2 * HEAD_DIM)
        for first in range(0, toks, ROWS):
            span = slice(first, first + ROWS)
            seen = None
            if masked:
                seen = ends <= base + first + lax.broadcasted_iota(jnp.int32, (ROWS, chunk), 0)
            for h in range(HEADS):
                cols = slice(h * HEAD_DIM, (h + 1) * HEAD_DIM)
                old = tuple(state[h, span, part] for part in PARTS)
                for part, new in zip(PARTS, fold(q_ref[span, cols], k, v, seen, old)):
                    state[h, span, part] = new

    def full(z, carry):
        step(z, False)
        return carry

    lax.fori_loop(0, pair, full, 0)
    step(pair, True)


def fine_kernel(
    meta, q_in, gw_in, part_in, state, a, b, s_a, s_b, near_ref, incoming, *refs
):
    out, q_ref, gw_ref, part_ref, c_keys, c_values, keys, values, done = refs[:9]
    in_sem, c_sem, sem, out_sem = refs[9:]
    toks = q_in.shape[0]
    first_loads = start_all([(q_in, q_ref), (gw_in, gw_ref), (part_in, part_ref)], in_sem)
    stretch, column, mine = unpack(meta)
    group = stretch * 8 + column
    half = a.shape[0]
    low, high = slice(0, half), slice(half, 2 * half)
    pairs = [(a, (low, 0)), (b, (high, 0)), (s_a, (low, 1)), (s_b, (high, 1))]
    loads = load_coarse(pairs, c_keys, c_values, c_sem)

    def fetch(i, run):
        owner = mine[i] >> 6
        place = pl.ds(i * SEL_BLOCK, SEL_BLOCK)

        def both(ref):
            to = values.at[place, pl.ds(0, HEAD_DIM)]
            run(pltpu.make_async_copy(ref.at[:, pl.ds(0, HEAD_DIM)], keys.at[place], sem.at[i]))
            run(pltpu.make_async_copy(ref.at[:, pl.ds(HEAD_DIM, HEAD_DIM)], to, sem.at[TOPN + i]))

        @pl.when(owner != stretch)
        def _():
            both(incoming.at[owner])

        @pl.when(owner == stretch)
        def _():
            both(near_ref.at[i])

    for i in range(TOPN):
        fetch(i, lambda copy: copy.start())
    fill_ones(values)
    lane = lax.broadcasted_iota(jnp.int32, (1, 2 * SEL_BLOCK), 1)
    pos = jnp.concatenate(
        [
            jnp.where(
                lane < SEL_BLOCK,
                mine[i] * SEL_BLOCK + lane,
                (mine[i + 1] - 1) * SEL_BLOCK + lane,
            )
            for i in range(0, TOPN, 2)
        ],
        axis=1,
    )
    for load in first_loads:
        load.wait()
    gates = gates_of(q_ref, gw_ref)
    chunk = 2 * half * len(FAR_SLOTS) * 64
    ends = coarse_ends(0, 2 * half, FAR_SLOTS, column)
    for load in loads:
        load.wait()
    for i in range(TOPN):
        fetch(i, lambda copy: copy.wait())
    c_k = c_keys[...].reshape(chunk, HEAD_DIM)
    c_v = c_values[...].reshape(chunk, 2 * HEAD_DIM)
    writes = []
    for first in range(0, toks, ROWS):
        span = slice(first, first + ROWS)
        base = group * toks + first
        place = base + lax.broadcasted_iota(jnp.int32, (ROWS, keys.shape[0]), 0)
        seen = pos <= place
        c_seen = ends <= place
        for h in range(HEADS):
            cols = slice(h * HEAD_DIM, (h + 1) * HEAD_DIM)
            old = tuple(state[h, span, part] for part in PARTS)
            acc, c_total, _ = fold(q_ref[span, cols], c_k, c_v, c_seen, old)
            o, total = attend(q_ref[span, cols], keys[...], values[...], seen)
            out_h = part_ref[span, cols] + acc * (gates[span, h : h + 1] / c_total)
            out_h += o * (gates[span, HEADS + h : HEADS + h + 1] / total)
            done[span, cols] = out_h.astype(done.dtype)
        write = pltpu.make_async_copy(done.at[span], out.at[span], out_sem.at[first // ROWS])
        write.start()
        writes.append(write)
    for write in writes:
        write.wait()


def hbm(x):
    return pltpu.with_memory_space_constraint(x, pltpu.MemorySpace.HBM)


def params(mib):
    return pltpu.CompilerParams(vmem_limit_bytes=mib << 20)


def solution(mesh):
    stretches = mesh.shape["blk"]
    group_size = mesh.shape["grp"]
    cores = 2
    ys = group_size // cores
    depth = 8
    up = route(stretches, ys, cores, lambda y, c: (y + 1, c))
    down = route(stretches, ys, cores, lambda y, c: (y - 1, c))
    swap = route(stretches, ys, cores, lambda y, c: (y, 1 - c))
    behind = [(i * group_size - 1, i * group_size) for i in range(1, stretches)]

    def cross(piece):
        return lax.ppermute(piece, AXES, swap)

    def spread(piece, ahead):
        half = piece.shape[0] // 2
        from1 = lax.ppermute(piece, AXES, up)
        from3 = lax.ppermute(piece, AXES, down)
        crossed = cross(piece)
        from1, from3, ahead = lax.optimization_barrier((from1, from3, ahead))
        far = (lax.ppermute(from1[:half], AXES, up), lax.ppermute(from3[half:], AXES, down))
        near = (piece, crossed, from1, cross(from1), from3, cross(from3))
        return near, far, ahead

    def per_device(
        queries, keys, values, selected, key_in, key_out, value_in, value_out, positions, gate_weight
    ):
        ids = jnp.stack([lax.axis_index("blk"), lax.axis_index("grp")]).astype(jnp.int32)
        ids, sel, keys, values, key_in, key_out, value_in, value_out, positions, queries, gate_weight = (
            hbm(x)
            for x in (
                ids,
                selected.T,
                keys,
                values,
                key_in,
                key_out,
                value_in,
                value_out,
                positions,
                queries,
                gate_weight.T,
            )
        )
        toks = queries.shape[0]
        per_dev = toks // SEL_BLOCK
        per_row = group_size * per_dev
        ncomp = toks // CMP_BLOCK
        per_z = stretches // depth * ncomp
        f32_rows = jax.ShapeDtypeStruct(queries.shape, jnp.float32)
        blocks = (SEL_BLOCK, 2 * HEAD_DIM)

        kv, meta = pl.pallas_call(
            prep_kernel,
            in_specs=[SMEM] + [HBM] * 3,
            out_specs=[VMEM] * 2,
            out_shape=[
                jax.ShapeDtypeStruct((toks, 2 * HEAD_DIM), jnp.bfloat16),
                jax.ShapeDtypeStruct((1, stretches * group_size + 128), jnp.int32),
            ],
            scratch_shapes=[
                pltpu.VMEM((2, toks, HEAD_DIM), jnp.bfloat16),
                pltpu.VMEM((TOPN, stretches * group_size), jnp.int32),
                pltpu.SemaphoreType.DMA((3,)),
            ],
            compiler_params=params(8),
            name="prep",
        )(ids, keys, values, sel)
        meta = hbm(meta)
        copies = pl.pallas_call(
            compress_kernel,
            in_specs=[HBM] * 7,
            out_specs=VMEM,
            out_shape=jax.ShapeDtypeStruct((stretches, ncomp, 2 * HEAD_DIM), jnp.bfloat16),
            scratch_shapes=[
                pltpu.VMEM((2, toks, HEAD_DIM), jnp.bfloat16),
                pltpu.VMEM(positions.shape, jnp.bfloat16),
                pltpu.VMEM((2, toks, HEAD_DIM), jnp.float32),
                pltpu.VMEM((2, ncomp, CMP_BLOCK * HEAD_DIM), jnp.bfloat16),
                pltpu.VMEM((2, *key_in.shape), jnp.bfloat16),
                pltpu.VMEM((2, *key_out.shape), jnp.bfloat16),
                pltpu.SemaphoreType.DMA((7,)),
            ],
            compiler_params=params(16),
            name="compress",
        )(keys, values, positions, key_in, key_out, value_in, value_out)
        near, far, copies = spread(kv.reshape(per_dev, *blocks), copies)
        edge = lax.ppermute(near[0], AXES, behind)
        s_own, s_from1 = near[1], near[3]
        copies, edge, _ = lax.optimization_barrier((copies, edge, (far, near[1], near[3], near[5])))
        column_comp = lax.all_to_all(copies, "blk", split_axis=0, concat_axis=0, tiled=True)
        outgoing, nearby = pl.pallas_call(
            pick_kernel,
            in_specs=[SMEM] + [ANY] * 10,
            out_specs=[HBM, HBM],
            out_shape=[
                jax.ShapeDtypeStruct((stretches, *blocks), jnp.bfloat16),
                jax.ShapeDtypeStruct((TOPN, *blocks), jnp.bfloat16),
            ],
            scratch_shapes=[
                pltpu.VMEM((per_row, *blocks), jnp.bfloat16),
                pltpu.SemaphoreType.DMA((stretches + TOPN,)),
            ],
            compiler_params=params(16),
            name="pick",
        )(meta, near[0], near[2], near[4], *far, near[1], near[3], near[5], *map(cross, far))
        incoming = lax.all_to_all(outgoing, "blk", split_axis=0, concat_axis=0, tiled=True)

        q_of = pltpu.VMEM(queries.shape, jnp.bfloat16)
        gw_of = pltpu.VMEM(gate_weight.shape, jnp.bfloat16)
        keys_of = pltpu.VMEM((2 * toks, HEAD_DIM), jnp.bfloat16)
        values_of = pltpu.VMEM((2 * toks, 2 * HEAD_DIM), jnp.bfloat16)
        flat = (toks, 2 * HEAD_DIM)
        local = pl.pallas_call(
            window_kernel,
            in_specs=[SMEM] + [HBM] * 2 + [ANY] * 4,
            out_specs=HBM,
            out_shape=f32_rows,
            scratch_shapes=[
                q_of,
                gw_of,
                pltpu.VMEM(queries.shape, jnp.float32),
                keys_of,
                values_of,
                pltpu.SemaphoreType.DMA((7,)),
            ],
            compiler_params=params(16),
            name="window",
        )(
            meta,
            queries,
            gate_weight,
            kv,
            s_own.reshape(flat),
            s_from1.reshape(flat),
            edge.reshape(flat),
        )

        column_comp = column_comp.reshape(depth, per_z, 2 * HEAD_DIM)
        comp_near, comp_far, local = spread(column_comp, local)

        def coarse_scratch(count):
            return [
                pltpu.VMEM((depth, count, per_z, HEAD_DIM), jnp.bfloat16),
                pltpu.VMEM((depth, count, per_z, 2 * HEAD_DIM), jnp.bfloat16),
            ]

        state = pl.pallas_call(
            near_kernel,
            in_specs=[SMEM] + [HBM] + [ANY] * 6,
            out_specs=VMEM,
            out_shape=jax.ShapeDtypeStruct((HEADS, toks, 3 * HEAD_DIM), jnp.float32),
            scratch_shapes=[q_of] + coarse_scratch(len(NEAR_SLOTS)) + [pltpu.SemaphoreType.DMA((13,))],
            compiler_params=params(20),
            name="near",
        )(meta, queries, *comp_near)
        comp_far, state = lax.optimization_barrier((comp_far, state))
        return pl.pallas_call(
            fine_kernel,
            in_specs=[SMEM] + [HBM] * 3 + [VMEM] + [HBM] * 5 + [ANY],
            out_specs=HBM,
            out_shape=jax.ShapeDtypeStruct(queries.shape, jnp.bfloat16),
            scratch_shapes=[q_of, gw_of, pltpu.VMEM(queries.shape, jnp.float32)]
            + coarse_scratch(len(FAR_SLOTS))
            + [
                keys_of,
                values_of,
                pltpu.VMEM(queries.shape, jnp.bfloat16),
                pltpu.SemaphoreType.DMA((3,)),
                pltpu.SemaphoreType.DMA((8,)),
                pltpu.SemaphoreType.DMA((2 * TOPN,)),
                pltpu.SemaphoreType.DMA((toks // ROWS,)),
            ],
            compiler_params=params(20),
            name="fine",
        )(
            meta,
            queries,
            gate_weight,
            hbm(local),
            state,
            *map(hbm, comp_far),
            *(hbm(cross(piece)) for piece in comp_far),
            hbm(nearby),
            incoming,
        )

    rows = P(AXES, None)
    return jax.shard_map(
        per_device,
        mesh=mesh,
        in_specs=(rows, rows, rows) + (P(),) * 7,
        out_specs=rows,
        check_vma=False,
    )
```

```python
import math

import jax
import jax.numpy as jnp
from jax import lax
from jax.experimental import pallas as pl
from jax.experimental.pallas import tpu as pltpu
from jax.sharding import PartitionSpec as P

HEAD_DIM = 128
HEADS = 4
CMP_BLOCK = 32
SEL_BLOCK = 64
TOPN = 16
WINDOW = 512
NEG = -1e30
SCALE2 = HEAD_DIM**-0.5 * math.log2(math.e)
AXES = ("blk", "grp")
ANY = pl.BlockSpec(memory_space=pl.ANY)
HBM = pl.BlockSpec(memory_space=pltpu.MemorySpace.HBM)
SMEM = pl.BlockSpec(memory_space=pltpu.SMEM)
VMEM = pl.BlockSpec(memory_space=pltpu.VMEM)


def route(stretches, rows, cores, move):
    pairs = []
    for b in range(stretches):
        for y in range(rows):
            for c in range(cores):
                to_y, to_c = move(y, c)
                pairs.append(((b * rows + y) * cores + c, (b * rows + to_y % rows) * cores + to_c))
    return pairs


def dot_t(a, b):
    return lax.dot_general(a, b, (((1,), (1,)), ((), ())), preferred_element_type=jnp.float32)


def lane_groups(x, op):
    parts = [x[:, i : i + 128] for i in range(0, x.shape[1], 128)]
    while len(parts) > 1:
        parts = [
            op(parts[i], parts[i + 1]) if i + 1 < len(parts) else parts[i]
            for i in range(0, len(parts), 2)
        ]
    return parts[0]


def gates_of(q_ref, gw_ref):
    return jax.nn.sigmoid(dot_t(q_ref[...], gw_ref[...]))


def start_all(pairs, sem):
    copies = [pltpu.make_async_copy(s, d, sem.at[i]) for i, (s, d) in enumerate(pairs)]
    for copy in copies:
        copy.start()
    return copies


def copy_all(pairs, sem):
    for copy in start_all(pairs, sem):
        copy.wait()


def prep_kernel(ids, keys_ref, values_ref, sel_ref, kv_ref, meta_ref, raw, sel_buf, sem):
    copy_all([(keys_ref, raw.at[0]), (values_ref, raw.at[1]), (sel_ref, sel_buf)], sem)
    kv_ref[:, :HEAD_DIM] = raw[0]
    kv_ref[:, HEAD_DIM:] = raw[1]
    sel = sel_buf[...]
    groups = sel.shape[1]
    group = lax.broadcasted_iota(jnp.int32, sel.shape, 1)
    match = ((sel >> 6) == ids[0]) & ((group >> 3) != ids[0])
    slot = slot_of(sel & 63, ids[1])
    meta_ref[:, :groups] = jnp.sum(jnp.where(match, slot, 0), axis=0, keepdims=True)
    mine = jnp.sum(jnp.where(group == ids[0] * 8 + ids[1], sel, 0), axis=1, keepdims=True)
    lane = lax.broadcasted_iota(jnp.int32, (TOPN, 128), 1)
    entry = lax.broadcasted_iota(jnp.int32, (TOPN, 128), 0)
    row = jnp.sum(jnp.where(lane == entry, mine, 0), axis=0, keepdims=True)
    row = jnp.where(lane[:1] == TOPN, ids[0], row)
    meta_ref[:, groups:] = jnp.where(lane[:1] == TOPN + 1, ids[1], row)


def unpack(meta):
    return meta[0, 256 + TOPN], meta[0, 257 + TOPN], [meta[0, 256 + i] for i in range(TOPN)]


def slot_of(block, column):
    owner = block >> 3
    dy = ((column >> 1) - (owner >> 1)) & 3
    return (((dy << 1) + ((owner ^ column) & 1)) << 3) + (block & 7)


def compress_kernel(
    keys_ref, values_ref, pos_ref, k_in, k_out, v_in, v_out, out_ref, raw, pos, wide, flat, w1, w2, sem
):
    toks = keys_ref.shape[0]
    count = toks // CMP_BLOCK
    loads = start_all(
        [
            (keys_ref, raw.at[0]),
            (pos_ref, pos),
            (values_ref, raw.at[1]),
            (k_in, w1.at[0]),
            (k_out, w2.at[0]),
            (v_in, w1.at[1]),
            (v_out, w2.at[1]),
        ],
        sem,
    )
    for load in loads[:3]:
        load.wait()
    for side in range(2):
        shift = pos[side].astype(jnp.float32)
        x = raw[side].astype(jnp.float32).reshape(count, CMP_BLOCK, HEAD_DIM) + shift[None]
        wide[side] = x.reshape(toks, HEAD_DIM)
        for t in range(CMP_BLOCK):
            rows = wide[side, pl.ds(t, count, stride=CMP_BLOCK), :]
            flat[side, :, t * HEAD_DIM : (t + 1) * HEAD_DIM] = rows.astype(jnp.bfloat16)
    for side in range(2):
        for load in loads[3 + 2 * side : 5 + 2 * side]:
            load.wait()
        hidden = jnp.dot(flat[side], w1[side], preferred_element_type=jnp.float32)
        hidden = (hidden * jax.nn.sigmoid(hidden)).astype(jnp.bfloat16)
        comp = jnp.dot(hidden, w2[side], preferred_element_type=jnp.float32).astype(jnp.bfloat16)
        cols = slice(side * HEAD_DIM, (side + 1) * HEAD_DIM)
        out_ref[:, :, cols] = jnp.broadcast_to(comp[None], (out_ref.shape[0], count, HEAD_DIM))


def pick_kernel(meta, *refs):
    out, nearby, rows, sem = refs[8:]
    copy_all([(ref, rows.at[pl.ds(i * 8, 8)]) for i, ref in enumerate(refs[:8])], sem)
    stretch, column, mine = unpack(meta)
    pairs = [(rows.at[meta[0, i * 8 + column]], out.at[i]) for i in range(out.shape[0])]
    for i in range(TOPN):
        pairs.append((rows.at[slot_of(mine[i] & 63, column)], nearby.at[i]))
    copy_all(pairs, sem)


def ones_beside(kv):
    kv[..., 2 * HEAD_DIM :] = jnp.ones((*kv.shape[:-1], HEAD_DIM), kv.dtype)


def attend(q, keys, values, seen):
    s = dot_t(q, keys)
    if seen is not None:
        s = jnp.where(seen, s, NEG)
    top = jnp.max(lane_groups(s, jnp.maximum), axis=1, keepdims=True)
    p = jnp.exp2((s - top) * SCALE2).astype(jnp.bfloat16)
    o = jnp.dot(p, values, preferred_element_type=jnp.float32)
    return o[:, :HEAD_DIM], o[:, HEAD_DIM:]


def window_kernel(
    meta, q_in, gw_in, kv_in, s_own, s_from1, edge, out, q_ref, gw_ref, out_ref, both, sem
):
    toks = q_in.shape[0]
    near, here = pl.ds(0, toks), pl.ds(toks, toks)
    front = pl.ds(0, 2 * HEAD_DIM)
    loads = start_all(
        [(q_in, q_ref), (gw_in, gw_ref), (kv_in, both.at[here, front])], sem.at[pl.ds(2, 3)]
    )
    stretch, column, _ = unpack(meta)

    @pl.when(column % 2 == 1)
    def _():
        copy_all([(s_own, both.at[near, front])], sem)

    @pl.when((column % 2 == 0) & (column > 0))
    def _():
        copy_all([(s_from1, both.at[near, front])], sem)

    @pl.when(column == 0)
    def _():
        copy_all([(edge, both.at[near, front])], sem)

    ones_beside(both)
    for load in loads:
        load.wait()
    low = jnp.where(stretch * 8 + column == 0, toks, 0)
    gates = gates_of(q_ref, gw_ref)
    rows = 128
    for first in range(0, toks, rows):
        span = slice(first, first + WINDOW + rows)
        r = lax.broadcasted_iota(jnp.int32, (rows, WINDOW + rows), 0)
        c = lax.broadcasted_iota(jnp.int32, (rows, WINDOW + rows), 1)
        seen = (c > r) & (c <= r + WINDOW) & (c + first >= low)
        for h in range(HEADS):
            cols = slice(h * HEAD_DIM, (h + 1) * HEAD_DIM)
            o, total = attend(
                q_ref[first : first + rows, cols], both[span, :HEAD_DIM], both[span, HEAD_DIM:], seen
            )
            g = gates[first : first + rows, 2 * HEADS + h : 2 * HEADS + h + 1]
            out_ref[first : first + rows, cols] = o * (g / total)
    copy_all([(out_ref, out)], sem)


SLOTS = ((0, 0), (0, 1), (1, 0), (1, 1), (2, 0), (2, 1), (3, 0), (3, 1))


def coarse_ends(stretch_z, zs, slots, column):
    lane = lax.broadcasted_iota(jnp.int32, (1, zs * len(slots) * 64), 1)
    z = jnp.zeros_like(lane)
    for i in range(1, zs):
        z += (lane >= i * len(slots) * 64).astype(jnp.int32)
    place = (lane >> 6) - z * len(slots)
    owner = jnp.zeros_like(lane)
    for i, (dy, dc) in enumerate(slots):
        theirs = ((((column >> 1) - dy) & 3) << 1) + ((column ^ dc) & 1)
        owner = jnp.where(place == i, theirs, owner)
    blk = ((stretch_z + z) << 2) + ((lane >> 4) & 3)
    return (((blk << 3) + owner) * 16 + (lane & 15)) * CMP_BLOCK + (CMP_BLOCK - 1)


def fold(q, keys, values, seen, old):
    s = dot_t(q, keys)
    if seen is not None:
        s = jnp.where(seen, s, NEG)
    acc, total, best = old
    top = jnp.maximum(best, jnp.max(lane_groups(s, jnp.maximum), axis=1, keepdims=True))
    wide = jnp.concatenate([top] * (s.shape[1] // 128), axis=1)
    p = jnp.exp2((s - wide) * SCALE2).astype(jnp.bfloat16)
    factor = jnp.exp2((best - top) * SCALE2)
    o = jnp.dot(p, values, preferred_element_type=jnp.float32)
    return acc * factor + o[:, :HEAD_DIM], total * factor + o[:, HEAD_DIM:], top


ROWS = 128
WIDE = 256
STEP = 4
PARTS = (slice(0, 128), slice(128, 256), slice(256, 384))


def coarse_kernel(meta, q_in, gw_in, local_in, *refs):
    pieces = refs[: len(SLOTS)]
    out_ref, q_ref, gw_ref, local, kv, state, sem = refs[len(SLOTS) :]
    stretch, column, _ = unpack(meta)
    toks = q_in.shape[0]
    pairs = [(ref, kv.at[:, i, :, pl.ds(0, 2 * HEAD_DIM)]) for i, ref in enumerate(pieces)]
    loads = start_all([(q_in, q_ref), (gw_in, gw_ref), *pairs, (local_in, local)], sem)
    ones_beside(kv)
    state[:, :, PARTS[0]] = jnp.zeros((HEADS, toks, 128), jnp.float32)
    state[:, :, PARTS[1]] = jnp.ones((HEADS, toks, 128), jnp.float32)
    state[:, :, PARTS[2]] = jnp.zeros((HEADS, toks, 128), jnp.float32)
    for load in loads[:-1]:
        load.wait()
    last = stretch >> 4
    chunk = STEP * len(SLOTS) * 64
    ends = coarse_ends(last * STEP, STEP, SLOTS, column)
    base = (stretch * 8 + column) * toks

    def step(z, masked):
        both = kv[pl.ds(STEP * z, STEP)].reshape(chunk, 3 * HEAD_DIM)
        k, v = both[:, :HEAD_DIM], both[:, HEAD_DIM:]
        for first in range(0, toks, ROWS):
            span = slice(first, first + ROWS)
            seen = None
            if masked:
                seen = ends <= base + first + lax.broadcasted_iota(jnp.int32, (ROWS, chunk), 0)
            for h in range(HEADS):
                cols = slice(h * HEAD_DIM, (h + 1) * HEAD_DIM)
                old = tuple(state[h, span, part] for part in PARTS)
                for part, new in zip(PARTS, fold(q_ref[span, cols], k, v, seen, old)):
                    state[h, span, part] = new

    def full(z, carry):
        step(z, False)
        return carry

    lax.fori_loop(0, last, full, 0)
    step(last, True)
    loads[-1].wait()
    gates = gates_of(q_ref, gw_ref)
    for h in range(HEADS):
        cols = slice(h * HEAD_DIM, (h + 1) * HEAD_DIM)
        acc, total = state[h, :, PARTS[0]], state[h, :, PARTS[1]]
        out_ref[:, cols] = local[:, cols] + acc * (gates[:, h : h + 1] / total)


def fine_kernel(
    meta, q_in, gw_in, part_ref, near_ref, incoming, *refs
):
    out, q_ref, gw_ref, kv, done, in_sem, sem, out_sem = refs
    toks = q_in.shape[0]
    loads = start_all([(q_in, q_ref), (gw_in, gw_ref)], in_sem)
    stretch, column, mine = unpack(meta)
    group = stretch * 8 + column

    def fetch(i, run):
        owner = mine[i] >> 6
        place = kv.at[pl.ds(i * SEL_BLOCK, SEL_BLOCK), pl.ds(0, 2 * HEAD_DIM)]

        @pl.when(owner != stretch)
        def _():
            run(pltpu.make_async_copy(incoming.at[owner], place, sem.at[i]))

        @pl.when(owner == stretch)
        def _():
            run(pltpu.make_async_copy(near_ref.at[i], place, sem.at[i]))

    for i in range(TOPN):
        fetch(i, lambda copy: copy.start())
    ones_beside(kv)
    lane = lax.broadcasted_iota(jnp.int32, (1, 2 * SEL_BLOCK), 1)
    pos = jnp.concatenate(
        [
            jnp.where(
                lane < SEL_BLOCK,
                mine[i] * SEL_BLOCK + lane,
                (mine[i + 1] - 1) * SEL_BLOCK + lane,
            )
            for i in range(0, TOPN, 2)
        ],
        axis=1,
    )
    for load in loads:
        load.wait()
    gates = gates_of(q_ref, gw_ref)
    for i in range(TOPN):
        fetch(i, lambda copy: copy.wait())
    writes = []
    for first in range(0, toks, WIDE):
        span = slice(first, first + WIDE)
        place = group * toks + first + lax.broadcasted_iota(jnp.int32, (WIDE, kv.shape[0]), 0)
        seen = pos <= place
        for h in range(HEADS):
            cols = slice(h * HEAD_DIM, (h + 1) * HEAD_DIM)
            o, total = attend(q_ref[span, cols], kv[:, :HEAD_DIM], kv[:, HEAD_DIM:], seen)
            g = gates[span, HEADS + h : HEADS + h + 1]
            done[span, cols] = (part_ref[span, cols] + o * (g / total)).astype(done.dtype)
        write = pltpu.make_async_copy(done.at[span], out.at[span], out_sem.at[first // WIDE])
        write.start()
        writes.append(write)
    for write in writes:
        write.wait()


def hbm(x):
    return pltpu.with_memory_space_constraint(x, pltpu.MemorySpace.HBM)


def params(mib):
    return pltpu.CompilerParams(vmem_limit_bytes=mib << 20)


def solution(mesh):
    stretches = mesh.shape["blk"]
    group_size = mesh.shape["grp"]
    cores = 2
    ys = group_size // cores
    depth = 8
    up = route(stretches, ys, cores, lambda y, c: (y + 1, c))
    down = route(stretches, ys, cores, lambda y, c: (y - 1, c))
    across = route(stretches, ys, cores, lambda y, c: (y + 2, c))
    swap = route(stretches, ys, cores, lambda y, c: (y, 1 - c))
    behind = [(i * group_size - 1, i * group_size) for i in range(1, stretches)]

    def cross(piece):
        return lax.ppermute(piece, AXES, swap)

    def spread(piece):
        return [lax.ppermute(piece, AXES, path) for path in (up, down, across)]

    def per_device(
        queries, keys, values, selected, key_in, key_out, value_in, value_out, positions, gate_weight
    ):
        ids = jnp.stack([lax.axis_index("blk"), lax.axis_index("grp")]).astype(jnp.int32)
        ids, sel, keys, values, key_in, key_out, value_in, value_out, positions, queries, gate_weight = (
            hbm(x)
            for x in (
                ids,
                selected.T,
                keys,
                values,
                key_in,
                key_out,
                value_in,
                value_out,
                positions,
                queries,
                gate_weight.T,
            )
        )
        toks = queries.shape[0]
        per_dev = toks // SEL_BLOCK
        per_row = group_size * per_dev
        ncomp = toks // CMP_BLOCK
        per_z = stretches // depth * ncomp
        f32_rows = jax.ShapeDtypeStruct(queries.shape, jnp.float32)
        blocks = (SEL_BLOCK, 2 * HEAD_DIM)

        kv, meta = pl.pallas_call(
            prep_kernel,
            in_specs=[SMEM] + [HBM] * 3,
            out_specs=[VMEM] * 2,
            out_shape=[
                jax.ShapeDtypeStruct((toks, 2 * HEAD_DIM), jnp.bfloat16),
                jax.ShapeDtypeStruct((1, stretches * group_size + 128), jnp.int32),
            ],
            scratch_shapes=[
                pltpu.VMEM((2, toks, HEAD_DIM), jnp.bfloat16),
                pltpu.VMEM((TOPN, stretches * group_size), jnp.int32),
                pltpu.SemaphoreType.DMA((3,)),
            ],
            compiler_params=params(8),
            name="prep",
        )(ids, keys, values, sel)
        meta = hbm(meta)
        copies = pl.pallas_call(
            compress_kernel,
            in_specs=[HBM] * 7,
            out_specs=VMEM,
            out_shape=jax.ShapeDtypeStruct((stretches, ncomp, 2 * HEAD_DIM), jnp.bfloat16),
            scratch_shapes=[
                pltpu.VMEM((2, toks, HEAD_DIM), jnp.bfloat16),
                pltpu.VMEM(positions.shape, jnp.bfloat16),
                pltpu.VMEM((2, toks, HEAD_DIM), jnp.float32),
                pltpu.VMEM((2, ncomp, CMP_BLOCK * HEAD_DIM), jnp.bfloat16),
                pltpu.VMEM((2, *key_in.shape), jnp.bfloat16),
                pltpu.VMEM((2, *key_out.shape), jnp.bfloat16),
                pltpu.SemaphoreType.DMA((7,)),
            ],
            compiler_params=params(16),
            name="compress",
        )(keys, values, positions, key_in, key_out, value_in, value_out)
        own = kv.reshape(per_dev, *blocks)
        s_own = cross(own)
        from1, from3, far = spread(own)
        edge = lax.ppermute(own, AXES, behind)
        copies, edge, s_own = lax.optimization_barrier((copies, edge, s_own))
        column_comp = lax.all_to_all(copies, "blk", split_axis=0, concat_axis=0, tiled=True)
        s_from1, s_from3, s_far = cross(from1), cross(from3), cross(far)

        outgoing, nearby = pl.pallas_call(
            pick_kernel,
            in_specs=[SMEM] + [ANY] * 8,
            out_specs=[HBM, HBM],
            out_shape=[
                jax.ShapeDtypeStruct((stretches, *blocks), jnp.bfloat16),
                jax.ShapeDtypeStruct((TOPN, *blocks), jnp.bfloat16),
            ],
            scratch_shapes=[
                pltpu.VMEM((per_row, *blocks), jnp.bfloat16),
                pltpu.SemaphoreType.DMA((stretches + TOPN,)),
            ],
            compiler_params=params(16),
            name="pick",
        )(meta, own, s_own, from1, s_from1, far, s_far, from3, s_from3)
        incoming = lax.all_to_all(outgoing, "blk", split_axis=0, concat_axis=0, tiled=True)

        q_of = pltpu.VMEM(queries.shape, jnp.bfloat16)
        gw_of = pltpu.VMEM(gate_weight.shape, jnp.bfloat16)
        kv_of = pltpu.VMEM((2 * toks, 3 * HEAD_DIM), jnp.bfloat16)
        flat = (toks, 2 * HEAD_DIM)
        local = pl.pallas_call(
            window_kernel,
            in_specs=[SMEM] + [HBM] * 2 + [ANY] * 4,
            out_specs=HBM,
            out_shape=f32_rows,
            scratch_shapes=[
                q_of,
                gw_of,
                pltpu.VMEM(queries.shape, jnp.float32),
                kv_of,
                pltpu.SemaphoreType.DMA((5,)),
            ],
            compiler_params=params(16),
            name="window",
        )(
            meta,
            queries,
            gate_weight,
            kv,
            s_own.reshape(flat),
            s_from1.reshape(flat),
            edge.reshape(flat),
        )

        own_comp = column_comp.reshape(depth, per_z, 2 * HEAD_DIM)
        comp1, comp3, comp_far = spread(own_comp)
        comp1, comp3, local = lax.optimization_barrier((comp1, comp3, local))
        pieces = (own_comp, comp1, comp_far, comp3)

        part = pl.pallas_call(
            coarse_kernel,
            in_specs=[SMEM] + [HBM] * 3 + [ANY] * 8,
            out_specs=VMEM,
            out_shape=f32_rows,
            scratch_shapes=[
                q_of,
                gw_of,
                pltpu.VMEM(queries.shape, jnp.float32),
                pltpu.VMEM((depth, group_size, per_z, 3 * HEAD_DIM), jnp.bfloat16),
                pltpu.VMEM((HEADS, toks, 3 * HEAD_DIM), jnp.float32),
                pltpu.SemaphoreType.DMA((11,)),
            ],
            compiler_params=params(24),
            name="coarse",
        )(meta, queries, gate_weight, hbm(local), *(x for piece in pieces for x in (piece, cross(piece))))

        return pl.pallas_call(
            fine_kernel,
            in_specs=[SMEM] + [HBM] * 2 + [VMEM, HBM, ANY],
            out_specs=HBM,
            out_shape=jax.ShapeDtypeStruct(queries.shape, jnp.bfloat16),
            scratch_shapes=[
                q_of,
                gw_of,
                kv_of,
                pltpu.VMEM(queries.shape, jnp.bfloat16),
                pltpu.SemaphoreType.DMA((2,)),
                pltpu.SemaphoreType.DMA((TOPN,)),
                pltpu.SemaphoreType.DMA((toks // WIDE,)),
            ],
            compiler_params=params(20),
            name="fine",
        )(meta, queries, gate_weight, part, hbm(nearby), incoming)

    rows = P(AXES, None)
    return jax.shard_map(
        per_device,
        mesh=mesh,
        in_specs=(rows, rows, rows) + (P(),) * 7,
        out_specs=rows,
        check_vma=False,
    )
```

```python
import math

import jax
import jax.numpy as jnp
from jax import lax
from jax.experimental import pallas as pl
from jax.experimental.pallas import tpu as pltpu
from jax.sharding import PartitionSpec as P

HEAD_DIM = 128
HEADS = 4
CMP_BLOCK = 32
SEL_BLOCK = 64
TOPN = 16
WINDOW = 512
NEG = -1e30
SCALE2 = HEAD_DIM**-0.5 * math.log2(math.e)
AXES = ("blk", "grp")
ANY = pl.BlockSpec(memory_space=pl.ANY)
HBM = pl.BlockSpec(memory_space=pltpu.MemorySpace.HBM)
SMEM = pl.BlockSpec(memory_space=pltpu.SMEM)
VMEM = pl.BlockSpec(memory_space=pltpu.VMEM)


def route(stretches, rows, cores, move):
    pairs = []
    for b in range(stretches):
        for y in range(rows):
            for c in range(cores):
                to_y, to_c = move(y, c)
                pairs.append(((b * rows + y) * cores + c, (b * rows + to_y % rows) * cores + to_c))
    return pairs


def dot_t(a, b):
    return lax.dot_general(a, b, (((1,), (1,)), ((), ())), preferred_element_type=jnp.float32)


def lane_groups(x, op):
    parts = [x[:, i : i + 128] for i in range(0, x.shape[1], 128)]
    while len(parts) > 1:
        parts = [
            op(parts[i], parts[i + 1]) if i + 1 < len(parts) else parts[i]
            for i in range(0, len(parts), 2)
        ]
    return parts[0]


def gates_of(q_ref, gw_ref):
    return jax.nn.sigmoid(dot_t(q_ref[...], gw_ref[...]))


def start_all(pairs, sem):
    copies = [pltpu.make_async_copy(s, d, sem.at[i]) for i, (s, d) in enumerate(pairs)]
    for copy in copies:
        copy.start()
    return copies


def copy_all(pairs, sem):
    for copy in start_all(pairs, sem):
        copy.wait()


def prep_kernel(ids, keys_ref, values_ref, sel_ref, kv_ref, meta_ref, raw, sel_buf, sem):
    copy_all([(keys_ref, raw.at[0]), (values_ref, raw.at[1]), (sel_ref, sel_buf)], sem)
    kv_ref[:, :HEAD_DIM] = raw[0]
    kv_ref[:, HEAD_DIM:] = raw[1]
    sel = sel_buf[...]
    groups = sel.shape[1]
    group = lax.broadcasted_iota(jnp.int32, sel.shape, 1)
    match = ((sel >> 6) == ids[0]) & ((group >> 3) != ids[0])
    slot = slot_of(sel & 63, ids[1])
    meta_ref[:, :groups] = jnp.sum(jnp.where(match, slot, 0), axis=0, keepdims=True)
    mine = jnp.sum(jnp.where(group == ids[0] * 8 + ids[1], sel, 0), axis=1, keepdims=True)
    lane = lax.broadcasted_iota(jnp.int32, (TOPN, 128), 1)
    entry = lax.broadcasted_iota(jnp.int32, (TOPN, 128), 0)
    row = jnp.sum(jnp.where(lane == entry, mine, 0), axis=0, keepdims=True)
    row = jnp.where(lane[:1] == TOPN, ids[0], row)
    meta_ref[:, groups:] = jnp.where(lane[:1] == TOPN + 1, ids[1], row)


def unpack(meta):
    return meta[0, 256 + TOPN], meta[0, 257 + TOPN], [meta[0, 256 + i] for i in range(TOPN)]


def slot_of(block, column):
    owner = block >> 3
    dy = ((column >> 1) - (owner >> 1)) & 3
    return (((dy << 1) + ((owner ^ column) & 1)) << 3) + (block & 7)


def compress_kernel(
    keys_ref, values_ref, pos_ref, k_in, k_out, v_in, v_out, out_ref, raw, pos, wide, flat, w1, w2, sem
):
    toks = keys_ref.shape[0]
    count = toks // CMP_BLOCK
    loads = start_all(
        [
            (keys_ref, raw.at[0]),
            (pos_ref, pos),
            (values_ref, raw.at[1]),
            (k_in, w1.at[0]),
            (k_out, w2.at[0]),
            (v_in, w1.at[1]),
            (v_out, w2.at[1]),
        ],
        sem,
    )
    for load in loads[:3]:
        load.wait()
    for side in range(2):
        shift = pos[side].astype(jnp.float32)
        x = raw[side].astype(jnp.float32).reshape(count, CMP_BLOCK, HEAD_DIM) + shift[None]
        wide[side] = x.reshape(toks, HEAD_DIM)
        for t in range(CMP_BLOCK):
            rows = wide[side, pl.ds(t, count, stride=CMP_BLOCK), :]
            flat[side, :, t * HEAD_DIM : (t + 1) * HEAD_DIM] = rows.astype(jnp.bfloat16)
    for side in range(2):
        for load in loads[3 + 2 * side : 5 + 2 * side]:
            load.wait()
        hidden = jnp.dot(flat[side], w1[side], preferred_element_type=jnp.float32)
        hidden = (hidden * jax.nn.sigmoid(hidden)).astype(jnp.bfloat16)
        comp = jnp.dot(hidden, w2[side], preferred_element_type=jnp.float32).astype(jnp.bfloat16)
        cols = slice(side * HEAD_DIM, (side + 1) * HEAD_DIM)
        out_ref[:, :, cols] = jnp.broadcast_to(comp[None], (out_ref.shape[0], count, HEAD_DIM))


def pick_kernel(meta, *refs):
    out, nearby, rows, sem = refs[8:]
    copy_all([(ref, rows.at[pl.ds(i * 8, 8)]) for i, ref in enumerate(refs[:8])], sem)
    stretch, column, mine = unpack(meta)
    pairs = [(rows.at[meta[0, i * 8 + column]], out.at[i]) for i in range(out.shape[0])]
    for i in range(TOPN):
        pairs.append((rows.at[slot_of(mine[i] & 63, column)], nearby.at[i]))
    copy_all(pairs, sem)


def ones_beside(kv):
    kv[..., 2 * HEAD_DIM :] = jnp.ones((*kv.shape[:-1], HEAD_DIM), kv.dtype)


def attend(q, keys, values, seen):
    s = dot_t(q, keys)
    if seen is not None:
        s = jnp.where(seen, s, NEG)
    top = jnp.max(lane_groups(s, jnp.maximum), axis=1, keepdims=True)
    p = jnp.exp2((s - top) * SCALE2).astype(jnp.bfloat16)
    o = jnp.dot(p, values, preferred_element_type=jnp.float32)
    return o[:, :HEAD_DIM], o[:, HEAD_DIM:]


def window_kernel(
    meta, q_in, gw_in, kv_in, s_own, s_from1, edge, out_ref, q_ref, gw_ref, both, sem
):
    toks = q_in.shape[0]
    near, here = pl.ds(0, toks), pl.ds(toks, toks)
    front = pl.ds(0, 2 * HEAD_DIM)
    loads = start_all(
        [(q_in, q_ref), (gw_in, gw_ref), (kv_in, both.at[here, front])], sem.at[pl.ds(2, 3)]
    )
    stretch, column, _ = unpack(meta)

    @pl.when(column % 2 == 1)
    def _():
        copy_all([(s_own, both.at[near, front])], sem)

    @pl.when((column % 2 == 0) & (column > 0))
    def _():
        copy_all([(s_from1, both.at[near, front])], sem)

    @pl.when(column == 0)
    def _():
        copy_all([(edge, both.at[near, front])], sem)

    ones_beside(both)
    for load in loads:
        load.wait()
    low = jnp.where(stretch * 8 + column == 0, toks, 0)
    gates = gates_of(q_ref, gw_ref)
    rows = 128
    for first in range(0, toks, rows):
        span = slice(first, first + WINDOW + rows)
        r = lax.broadcasted_iota(jnp.int32, (rows, WINDOW + rows), 0)
        c = lax.broadcasted_iota(jnp.int32, (rows, WINDOW + rows), 1)
        seen = (c > r) & (c <= r + WINDOW) & (c + first >= low)
        for h in range(HEADS):
            cols = slice(h * HEAD_DIM, (h + 1) * HEAD_DIM)
            o, total = attend(
                q_ref[first : first + rows, cols], both[span, :HEAD_DIM], both[span, HEAD_DIM:], seen
            )
            g = gates[first : first + rows, 2 * HEADS + h : 2 * HEADS + h + 1]
            out_ref[first : first + rows, cols] = o * (g / total)


SLOTS = ((0, 0), (0, 1), (1, 0), (1, 1), (2, 0), (2, 1), (3, 0), (3, 1))


def coarse_ends(stretch_z, zs, slots, column):
    lane = lax.broadcasted_iota(jnp.int32, (1, zs * len(slots) * 64), 1)
    z = jnp.zeros_like(lane)
    for i in range(1, zs):
        z += (lane >= i * len(slots) * 64).astype(jnp.int32)
    place = (lane >> 6) - z * len(slots)
    owner = jnp.zeros_like(lane)
    for i, (dy, dc) in enumerate(slots):
        theirs = ((((column >> 1) - dy) & 3) << 1) + ((column ^ dc) & 1)
        owner = jnp.where(place == i, theirs, owner)
    blk = ((stretch_z + z) << 2) + ((lane >> 4) & 3)
    return (((blk << 3) + owner) * 16 + (lane & 15)) * CMP_BLOCK + (CMP_BLOCK - 1)


def fold(q, keys, values, seen, old):
    s = dot_t(q, keys)
    if seen is not None:
        s = jnp.where(seen, s, NEG)
    acc, total, best = old
    top = jnp.maximum(best, jnp.max(lane_groups(s, jnp.maximum), axis=1, keepdims=True))
    wide = jnp.concatenate([top] * (s.shape[1] // 128), axis=1)
    p = jnp.exp2((s - wide) * SCALE2).astype(jnp.bfloat16)
    factor = jnp.exp2((best - top) * SCALE2)
    o = jnp.dot(p, values, preferred_element_type=jnp.float32)
    return acc * factor + o[:, :HEAD_DIM], total * factor + o[:, HEAD_DIM:], top


ROWS = 256
WIDE = 256
STEP = 4
PARTS = (slice(0, 128), slice(128, 256), slice(256, 384))


def coarse_kernel(meta, q_in, gw_in, local_in, *refs):
    pieces = refs[: len(SLOTS)]
    out_ref, q_ref, gw_ref, local, kv, state, sem = refs[len(SLOTS) :]
    stretch, column, _ = unpack(meta)
    toks = q_in.shape[0]
    pairs = [(ref, kv.at[:, i, :, pl.ds(0, 2 * HEAD_DIM)]) for i, ref in enumerate(pieces)]
    loads = start_all([(q_in, q_ref), (gw_in, gw_ref), *pairs, (local_in, local)], sem)
    ones_beside(kv)
    state[:, :, PARTS[0]] = jnp.zeros((HEADS, toks, 128), jnp.float32)
    state[:, :, PARTS[1]] = jnp.ones((HEADS, toks, 128), jnp.float32)
    state[:, :, PARTS[2]] = jnp.zeros((HEADS, toks, 128), jnp.float32)
    for load in loads[:-1]:
        load.wait()
    last = stretch >> 4
    chunk = STEP * len(SLOTS) * 64
    ends = coarse_ends(last * STEP, STEP, SLOTS, column)
    base = (stretch * 8 + column) * toks

    def step(z, masked):
        both = kv[pl.ds(STEP * z, STEP)].reshape(chunk, 3 * HEAD_DIM)
        k, v = both[:, :HEAD_DIM], both[:, HEAD_DIM:]
        for first in range(0, toks, ROWS):
            span = slice(first, first + ROWS)
            seen = None
            if masked:
                seen = ends <= base + first + lax.broadcasted_iota(jnp.int32, (ROWS, chunk), 0)
            for h in range(HEADS):
                cols = slice(h * HEAD_DIM, (h + 1) * HEAD_DIM)
                old = tuple(state[h, span, part] for part in PARTS)
                for part, new in zip(PARTS, fold(q_ref[span, cols], k, v, seen, old)):
                    state[h, span, part] = new

    def full(z, carry):
        step(z, False)
        return carry

    lax.fori_loop(0, last, full, 0)
    step(last, True)
    loads[-1].wait()
    gates = gates_of(q_ref, gw_ref)
    for h in range(HEADS):
        cols = slice(h * HEAD_DIM, (h + 1) * HEAD_DIM)
        acc, total = state[h, :, PARTS[0]], state[h, :, PARTS[1]]
        out_ref[:, cols] = local[:, cols] + acc * (gates[:, h : h + 1] / total)


def fine_kernel(
    meta, q_in, gw_in, part_ref, near_ref, incoming, *refs
):
    out, q_ref, gw_ref, kv, done, in_sem, sem, out_sem = refs
    toks = q_in.shape[0]
    loads = start_all([(q_in, q_ref), (gw_in, gw_ref)], in_sem)
    stretch, column, mine = unpack(meta)
    group = stretch * 8 + column

    def fetch(i, run):
        owner = mine[i] >> 6
        place = kv.at[pl.ds(i * SEL_BLOCK, SEL_BLOCK), pl.ds(0, 2 * HEAD_DIM)]

        @pl.when(owner != stretch)
        def _():
            run(pltpu.make_async_copy(incoming.at[owner], place, sem.at[i]))

        @pl.when(owner == stretch)
        def _():
            run(pltpu.make_async_copy(near_ref.at[i], place, sem.at[i]))

    for i in range(TOPN):
        fetch(i, lambda copy: copy.start())
    ones_beside(kv)
    lane = lax.broadcasted_iota(jnp.int32, (1, 2 * SEL_BLOCK), 1)
    pos = jnp.concatenate(
        [
            jnp.where(
                lane < SEL_BLOCK,
                mine[i] * SEL_BLOCK + lane,
                (mine[i + 1] - 1) * SEL_BLOCK + lane,
            )
            for i in range(0, TOPN, 2)
        ],
        axis=1,
    )
    for load in loads:
        load.wait()
    gates = gates_of(q_ref, gw_ref)
    for i in range(TOPN):
        fetch(i, lambda copy: copy.wait())
    writes = []
    for first in range(0, toks, WIDE):
        span = slice(first, first + WIDE)
        place = group * toks + first + lax.broadcasted_iota(jnp.int32, (WIDE, kv.shape[0]), 0)
        seen = pos <= place
        for h in range(HEADS):
            cols = slice(h * HEAD_DIM, (h + 1) * HEAD_DIM)
            o, total = attend(q_ref[span, cols], kv[:, :HEAD_DIM], kv[:, HEAD_DIM:], seen)
            g = gates[span, HEADS + h : HEADS + h + 1]
            done[span, cols] = (part_ref[span, cols] + o * (g / total)).astype(done.dtype)
        write = pltpu.make_async_copy(done.at[span], out.at[span], out_sem.at[first // WIDE])
        write.start()
        writes.append(write)
    for write in writes:
        write.wait()


def hbm(x):
    return pltpu.with_memory_space_constraint(x, pltpu.MemorySpace.HBM)


def params(mib):
    return pltpu.CompilerParams(vmem_limit_bytes=mib << 20)


def solution(mesh):
    stretches = mesh.shape["blk"]
    group_size = mesh.shape["grp"]
    cores = 2
    ys = group_size // cores
    depth = 8
    up = route(stretches, ys, cores, lambda y, c: (y + 1, c))
    down = route(stretches, ys, cores, lambda y, c: (y - 1, c))
    across = route(stretches, ys, cores, lambda y, c: (y + 2, c))
    swap = route(stretches, ys, cores, lambda y, c: (y, 1 - c))
    behind = [(i * group_size - 1, i * group_size) for i in range(1, stretches)]

    def cross(piece):
        return lax.ppermute(piece, AXES, swap)

    def spread(piece):
        return [lax.ppermute(piece, AXES, path) for path in (up, down, across)]

    def per_device(
        queries, keys, values, selected, key_in, key_out, value_in, value_out, positions, gate_weight
    ):
        ids = jnp.stack([lax.axis_index("blk"), lax.axis_index("grp")]).astype(jnp.int32)
        ids, sel, keys, values, key_in, key_out, value_in, value_out, positions, queries, gate_weight = (
            hbm(x)
            for x in (
                ids,
                selected.T,
                keys,
                values,
                key_in,
                key_out,
                value_in,
                value_out,
                positions,
                queries,
                gate_weight.T,
            )
        )
        toks = queries.shape[0]
        per_dev = toks // SEL_BLOCK
        per_row = group_size * per_dev
        ncomp = toks // CMP_BLOCK
        per_z = stretches // depth * ncomp
        f32_rows = jax.ShapeDtypeStruct(queries.shape, jnp.float32)
        blocks = (SEL_BLOCK, 2 * HEAD_DIM)

        kv, meta = pl.pallas_call(
            prep_kernel,
            in_specs=[SMEM] + [HBM] * 3,
            out_specs=[VMEM] * 2,
            out_shape=[
                jax.ShapeDtypeStruct((toks, 2 * HEAD_DIM), jnp.bfloat16),
                jax.ShapeDtypeStruct((1, stretches * group_size + 128), jnp.int32),
            ],
            scratch_shapes=[
                pltpu.VMEM((2, toks, HEAD_DIM), jnp.bfloat16),
                pltpu.VMEM((TOPN, stretches * group_size), jnp.int32),
                pltpu.SemaphoreType.DMA((3,)),
            ],
            compiler_params=params(8),
            name="prep",
        )(ids, keys, values, sel)
        meta = hbm(meta)
        copies = pl.pallas_call(
            compress_kernel,
            in_specs=[HBM] * 7,
            out_specs=VMEM,
            out_shape=jax.ShapeDtypeStruct((stretches, ncomp, 2 * HEAD_DIM), jnp.bfloat16),
            scratch_shapes=[
                pltpu.VMEM((2, toks, HEAD_DIM), jnp.bfloat16),
                pltpu.VMEM(positions.shape, jnp.bfloat16),
                pltpu.VMEM((2, toks, HEAD_DIM), jnp.float32),
                pltpu.VMEM((2, ncomp, CMP_BLOCK * HEAD_DIM), jnp.bfloat16),
                pltpu.VMEM((2, *key_in.shape), jnp.bfloat16),
                pltpu.VMEM((2, *key_out.shape), jnp.bfloat16),
                pltpu.SemaphoreType.DMA((7,)),
            ],
            compiler_params=params(16),
            name="compress",
        )(keys, values, positions, key_in, key_out, value_in, value_out)
        own = kv.reshape(per_dev, *blocks)
        s_own = cross(own)
        from1, from3, far = spread(own)
        edge = lax.ppermute(own, AXES, behind)
        copies, edge, s_own = lax.optimization_barrier((copies, edge, s_own))
        column_comp = lax.all_to_all(copies, "blk", split_axis=0, concat_axis=0, tiled=True)
        s_from1, s_from3, s_far = cross(from1), cross(from3), cross(far)

        outgoing, nearby = pl.pallas_call(
            pick_kernel,
            in_specs=[SMEM] + [ANY] * 8,
            out_specs=[HBM, HBM],
            out_shape=[
                jax.ShapeDtypeStruct((stretches, *blocks), jnp.bfloat16),
                jax.ShapeDtypeStruct((TOPN, *blocks), jnp.bfloat16),
            ],
            scratch_shapes=[
                pltpu.VMEM((per_row, *blocks), jnp.bfloat16),
                pltpu.SemaphoreType.DMA((stretches + TOPN,)),
            ],
            compiler_params=params(16),
            name="pick",
        )(meta, own, s_own, from1, s_from1, far, s_far, from3, s_from3)
        incoming = lax.all_to_all(outgoing, "blk", split_axis=0, concat_axis=0, tiled=True)

        q_of = pltpu.VMEM(queries.shape, jnp.bfloat16)
        gw_of = pltpu.VMEM(gate_weight.shape, jnp.bfloat16)
        kv_of = pltpu.VMEM((2 * toks, 3 * HEAD_DIM), jnp.bfloat16)
        flat = (toks, 2 * HEAD_DIM)
        local = pl.pallas_call(
            window_kernel,
            in_specs=[SMEM] + [HBM] * 2 + [ANY] * 4,
            out_specs=VMEM,
            out_shape=f32_rows,
            scratch_shapes=[
                q_of,
                gw_of,
                kv_of,
                pltpu.SemaphoreType.DMA((5,)),
            ],
            compiler_params=params(16),
            name="window",
        )(
            meta,
            queries,
            gate_weight,
            kv,
            s_own.reshape(flat),
            s_from1.reshape(flat),
            edge.reshape(flat),
        )

        own_comp = column_comp.reshape(depth, per_z, 2 * HEAD_DIM)
        comp1, comp3, comp_far = spread(own_comp)
        comp1, comp3, local = lax.optimization_barrier((comp1, comp3, local))
        pieces = (own_comp, comp1, comp_far, comp3)

        part = pl.pallas_call(
            coarse_kernel,
            in_specs=[SMEM] + [HBM] * 2 + [ANY] * 9,
            out_specs=VMEM,
            out_shape=f32_rows,
            scratch_shapes=[
                q_of,
                gw_of,
                pltpu.VMEM(queries.shape, jnp.float32),
                pltpu.VMEM((depth, group_size, per_z, 3 * HEAD_DIM), jnp.bfloat16),
                pltpu.VMEM((HEADS, toks, 3 * HEAD_DIM), jnp.float32),
                pltpu.SemaphoreType.DMA((11,)),
            ],
            compiler_params=params(24),
            name="coarse",
        )(meta, queries, gate_weight, local, *(x for piece in pieces for x in (piece, cross(piece))))

        return pl.pallas_call(
            fine_kernel,
            in_specs=[SMEM] + [HBM] * 2 + [VMEM, HBM, ANY],
            out_specs=HBM,
            out_shape=jax.ShapeDtypeStruct(queries.shape, jnp.bfloat16),
            scratch_shapes=[
                q_of,
                gw_of,
                kv_of,
                pltpu.VMEM(queries.shape, jnp.bfloat16),
                pltpu.SemaphoreType.DMA((2,)),
                pltpu.SemaphoreType.DMA((TOPN,)),
                pltpu.SemaphoreType.DMA((toks // WIDE,)),
            ],
            compiler_params=params(20),
            name="fine",
        )(meta, queries, gate_weight, part, hbm(nearby), incoming)

    rows = P(AXES, None)
    return jax.shard_map(
        per_device,
        mesh=mesh,
        in_specs=(rows, rows, rows) + (P(),) * 7,
        out_specs=rows,
        check_vma=False,
    )
```

```python
import math

import jax
import jax.numpy as jnp
from jax import lax
from jax.experimental import pallas as pl
from jax.experimental.pallas import tpu as pltpu
from jax.sharding import PartitionSpec as P

HEAD_DIM = 128
HEADS = 4
CMP_BLOCK = 32
SEL_BLOCK = 64
TOPN = 16
WINDOW = 512
NEG = -1e30
SCALE2 = HEAD_DIM**-0.5 * math.log2(math.e)
AXES = ("blk", "grp")
ANY = pl.BlockSpec(memory_space=pl.ANY)
HBM = pl.BlockSpec(memory_space=pltpu.MemorySpace.HBM)
SMEM = pl.BlockSpec(memory_space=pltpu.SMEM)
VMEM = pl.BlockSpec(memory_space=pltpu.VMEM)


def route(stretches, rows, cores, move):
    pairs = []
    for b in range(stretches):
        for y in range(rows):
            for c in range(cores):
                to_y, to_c = move(y, c)
                pairs.append(((b * rows + y) * cores + c, (b * rows + to_y % rows) * cores + to_c))
    return pairs


def dot_t(a, b):
    return lax.dot_general(a, b, (((1,), (1,)), ((), ())), preferred_element_type=jnp.float32)


def lane_groups(x, op):
    parts = [x[:, i : i + 128] for i in range(0, x.shape[1], 128)]
    while len(parts) > 1:
        parts = [
            op(parts[i], parts[i + 1]) if i + 1 < len(parts) else parts[i]
            for i in range(0, len(parts), 2)
        ]
    return parts[0]


def gates_of(q_ref, gw_ref):
    return jax.nn.sigmoid(dot_t(q_ref[...], gw_ref[...]))


def start_all(pairs, sem):
    copies = [pltpu.make_async_copy(s, d, sem.at[i]) for i, (s, d) in enumerate(pairs)]
    for copy in copies:
        copy.start()
    return copies


def copy_all(pairs, sem):
    for copy in start_all(pairs, sem):
        copy.wait()


def prep_kernel(ids, keys_ref, values_ref, sel_ref, kv_ref, meta_ref, raw, sel_buf, sem):
    copy_all([(keys_ref, raw.at[0]), (values_ref, raw.at[1]), (sel_ref, sel_buf)], sem)
    kv_ref[:, :HEAD_DIM] = raw[0]
    kv_ref[:, HEAD_DIM:] = raw[1]
    sel = sel_buf[...]
    groups = sel.shape[1]
    group = lax.broadcasted_iota(jnp.int32, sel.shape, 1)
    match = ((sel >> 6) == ids[0]) & ((group >> 3) != ids[0])
    slot = slot_of(sel & 63, ids[1])
    meta_ref[:, :groups] = jnp.sum(jnp.where(match, slot, 0), axis=0, keepdims=True)
    mine = jnp.sum(jnp.where(group == ids[0] * 8 + ids[1], sel, 0), axis=1, keepdims=True)
    lane = lax.broadcasted_iota(jnp.int32, (TOPN, 128), 1)
    entry = lax.broadcasted_iota(jnp.int32, (TOPN, 128), 0)
    row = jnp.sum(jnp.where(lane == entry, mine, 0), axis=0, keepdims=True)
    row = jnp.where(lane[:1] == TOPN, ids[0], row)
    meta_ref[:, groups:] = jnp.where(lane[:1] == TOPN + 1, ids[1], row)


def unpack(meta):
    return meta[0, 256 + TOPN], meta[0, 257 + TOPN], [meta[0, 256 + i] for i in range(TOPN)]


def slot_of(block, column):
    owner = block >> 3
    dy = ((column >> 1) - (owner >> 1)) & 3
    return (((dy << 1) + ((owner ^ column) & 1)) << 3) + (block & 7)


def compress_kernel(
    keys_ref, values_ref, pos_ref, k_in, k_out, v_in, v_out, out_ref, raw, pos, wide, flat, w1, w2, sem
):
    toks = keys_ref.shape[0]
    count = toks // CMP_BLOCK
    loads = start_all(
        [
            (keys_ref, raw.at[0]),
            (pos_ref, pos),
            (values_ref, raw.at[1]),
            (k_in, w1.at[0]),
            (k_out, w2.at[0]),
            (v_in, w1.at[1]),
            (v_out, w2.at[1]),
        ],
        sem,
    )
    for load in loads[:3]:
        load.wait()
    for side in range(2):
        shift = pos[side].astype(jnp.float32)
        x = raw[side].astype(jnp.float32).reshape(count, CMP_BLOCK, HEAD_DIM) + shift[None]
        wide[side] = x.reshape(toks, HEAD_DIM)
        for t in range(CMP_BLOCK):
            rows = wide[side, pl.ds(t, count, stride=CMP_BLOCK), :]
            flat[side, :, t * HEAD_DIM : (t + 1) * HEAD_DIM] = rows.astype(jnp.bfloat16)
    for side in range(2):
        for load in loads[3 + 2 * side : 5 + 2 * side]:
            load.wait()
        hidden = jnp.dot(flat[side], w1[side], preferred_element_type=jnp.float32)
        hidden = (hidden * jax.nn.sigmoid(hidden)).astype(jnp.bfloat16)
        comp = jnp.dot(hidden, w2[side], preferred_element_type=jnp.float32).astype(jnp.bfloat16)
        cols = slice(side * HEAD_DIM, (side + 1) * HEAD_DIM)
        out_ref[:, :, cols] = jnp.broadcast_to(comp[None], (out_ref.shape[0], count, HEAD_DIM))


def pick_kernel(meta, *refs):
    out, nearby, rows, sem = refs[8:]
    copy_all([(ref, rows.at[pl.ds(i * 8, 8)]) for i, ref in enumerate(refs[:8])], sem)
    stretch, column, mine = unpack(meta)
    pairs = [(rows.at[meta[0, i * 8 + column]], out.at[i]) for i in range(out.shape[0])]
    for i in range(TOPN):
        pairs.append((rows.at[slot_of(mine[i] & 63, column)], nearby.at[i]))
    copy_all(pairs, sem)


def ones_beside(kv):
    kv[..., 2 * HEAD_DIM :] = jnp.ones((*kv.shape[:-1], HEAD_DIM), kv.dtype)


def attend(q, keys, values, seen):
    s = dot_t(q, keys)
    if seen is not None:
        s = jnp.where(seen, s, NEG)
    top = jnp.max(lane_groups(s, jnp.maximum), axis=1, keepdims=True)
    p = jnp.exp2((s - top) * SCALE2).astype(jnp.bfloat16)
    o = jnp.dot(p, values, preferred_element_type=jnp.float32)
    return o[:, :HEAD_DIM], o[:, HEAD_DIM:]


def window_kernel(
    meta, q_in, gw_in, kv_in, s_own, s_from1, edge, out_ref, q_ref, gw_ref, both, sem
):
    toks = q_in.shape[0]
    near, here = pl.ds(0, toks), pl.ds(toks, toks)
    front = pl.ds(0, 2 * HEAD_DIM)
    loads = start_all(
        [(q_in, q_ref), (gw_in, gw_ref), (kv_in, both.at[here, front])], sem.at[pl.ds(2, 3)]
    )
    stretch, column, _ = unpack(meta)

    @pl.when(column % 2 == 1)
    def _():
        copy_all([(s_own, both.at[near, front])], sem)

    @pl.when((column % 2 == 0) & (column > 0))
    def _():
        copy_all([(s_from1, both.at[near, front])], sem)

    @pl.when(column == 0)
    def _():
        copy_all([(edge, both.at[near, front])], sem)

    ones_beside(both)
    for load in loads:
        load.wait()
    low = jnp.where(stretch * 8 + column == 0, toks, 0)
    gates = gates_of(q_ref, gw_ref)
    rows = 128
    for first in range(0, toks, rows):
        span = slice(first, first + WINDOW + rows)
        r = lax.broadcasted_iota(jnp.int32, (rows, WINDOW + rows), 0)
        c = lax.broadcasted_iota(jnp.int32, (rows, WINDOW + rows), 1)
        seen = (c > r) & (c <= r + WINDOW) & (c + first >= low)
        for h in range(HEADS):
            cols = slice(h * HEAD_DIM, (h + 1) * HEAD_DIM)
            o, total = attend(
                q_ref[first : first + rows, cols], both[span, :HEAD_DIM], both[span, HEAD_DIM:], seen
            )
            g = gates[first : first + rows, 2 * HEADS + h : 2 * HEADS + h + 1]
            out_ref[first : first + rows, cols] = o * (g / total)


SLOTS = ((0, 0), (0, 1), (1, 0), (1, 1), (2, 0), (2, 1), (3, 0), (3, 1))


def coarse_ends(stretch_z, zs, slots, column):
    lane = lax.broadcasted_iota(jnp.int32, (1, zs * len(slots) * 64), 1)
    z = jnp.zeros_like(lane)
    for i in range(1, zs):
        z += (lane >= i * len(slots) * 64).astype(jnp.int32)
    place = (lane >> 6) - z * len(slots)
    owner = jnp.zeros_like(lane)
    for i, (dy, dc) in enumerate(slots):
        theirs = ((((column >> 1) - dy) & 3) << 1) + ((column ^ dc) & 1)
        owner = jnp.where(place == i, theirs, owner)
    blk = ((stretch_z + z) << 2) + ((lane >> 4) & 3)
    return (((blk << 3) + owner) * 16 + (lane & 15)) * CMP_BLOCK + (CMP_BLOCK - 1)


def fold(q, keys, values, seen, old):
    s = dot_t(q, keys)
    if seen is not None:
        s = jnp.where(seen, s, NEG)
    acc, total, best = old
    top = jnp.maximum(best, jnp.max(lane_groups(s, jnp.maximum), axis=1, keepdims=True))
    wide = jnp.concatenate([top] * (s.shape[1] // 128), axis=1)
    p = jnp.exp2((s - wide) * SCALE2).astype(jnp.bfloat16)
    factor = jnp.exp2((best - top) * SCALE2)
    o = jnp.dot(p, values, preferred_element_type=jnp.float32)
    return acc * factor + o[:, :HEAD_DIM], total * factor + o[:, HEAD_DIM:], top


ROWS = 256
WIDE = 256
STEP = 4
PARTS = (slice(0, 128), slice(128, 256), slice(256, 384))


def coarse_kernel(meta, q_in, gw_in, local_in, *refs):
    pieces = refs[: len(SLOTS)]
    out_ref, q_ref, gw_ref, local, kv, state, sem = refs[len(SLOTS) :]
    stretch, column, _ = unpack(meta)
    toks = q_in.shape[0]
    pairs = [(ref, kv.at[:, i, :, pl.ds(0, 2 * HEAD_DIM)]) for i, ref in enumerate(pieces)]
    loads = start_all([(q_in, q_ref), (gw_in, gw_ref), *pairs, (local_in, local)], sem)
    ones_beside(kv)
    state[:, :, PARTS[0]] = jnp.zeros((HEADS, toks, 128), jnp.float32)
    state[:, :, PARTS[1]] = jnp.ones((HEADS, toks, 128), jnp.float32)
    state[:, :, PARTS[2]] = jnp.zeros((HEADS, toks, 128), jnp.float32)
    for load in loads[:-1]:
        load.wait()
    last = stretch >> 4
    chunk = STEP * len(SLOTS) * 64
    ends = coarse_ends(last * STEP, STEP, SLOTS, column)
    base = (stretch * 8 + column) * toks

    def step(z, masked):
        both = kv[pl.ds(STEP * z, STEP)].reshape(chunk, 3 * HEAD_DIM)
        k, v = both[:, :HEAD_DIM], both[:, HEAD_DIM:]
        for first in range(0, toks, ROWS):
            span = slice(first, first + ROWS)
            seen = None
            if masked:
                seen = ends <= base + first + lax.broadcasted_iota(jnp.int32, (ROWS, chunk), 0)
            for h in range(HEADS):
                cols = slice(h * HEAD_DIM, (h + 1) * HEAD_DIM)
                old = tuple(state[h, span, part] for part in PARTS)
                for part, new in zip(PARTS, fold(q_ref[span, cols], k, v, seen, old)):
                    state[h, span, part] = new

    def full(z, carry):
        step(z, False)
        return carry

    lax.fori_loop(0, last, full, 0)
    step(last, True)
    loads[-1].wait()
    gates = gates_of(q_ref, gw_ref)
    for h in range(HEADS):
        cols = slice(h * HEAD_DIM, (h + 1) * HEAD_DIM)
        acc, total = state[h, :, PARTS[0]], state[h, :, PARTS[1]]
        out_ref[:, cols] = local[:, cols] + acc * (gates[:, h : h + 1] / total)


def fine_kernel(
    meta, q_in, gw_in, part_ref, near_ref, incoming, *refs
):
    out, q_ref, gw_ref, kv, done, in_sem, sem, out_sem = refs
    toks = q_in.shape[0]
    loads = start_all([(q_in, q_ref), (gw_in, gw_ref)], in_sem)
    stretch, column, mine = unpack(meta)
    group = stretch * 8 + column

    def fetch(i, run):
        owner = mine[i] >> 6
        place = kv.at[pl.ds(i * SEL_BLOCK, SEL_BLOCK), pl.ds(0, 2 * HEAD_DIM)]

        @pl.when(owner != stretch)
        def _():
            run(pltpu.make_async_copy(incoming.at[owner], place, sem.at[i]))

        @pl.when(owner == stretch)
        def _():
            run(pltpu.make_async_copy(near_ref.at[i], place, sem.at[i]))

    for i in range(TOPN):
        fetch(i, lambda copy: copy.start())
    ones_beside(kv)
    lane = lax.broadcasted_iota(jnp.int32, (1, 2 * SEL_BLOCK), 1)
    pos = jnp.concatenate(
        [
            jnp.where(
                lane < SEL_BLOCK,
                mine[i] * SEL_BLOCK + lane,
                (mine[i + 1] - 1) * SEL_BLOCK + lane,
            )
            for i in range(0, TOPN, 2)
        ],
        axis=1,
    )
    for load in loads:
        load.wait()
    gates = gates_of(q_ref, gw_ref)
    for i in range(TOPN):
        fetch(i, lambda copy: copy.wait())
    writes = []
    for first in range(0, toks, WIDE):
        span = slice(first, first + WIDE)
        place = group * toks + first + lax.broadcasted_iota(jnp.int32, (WIDE, kv.shape[0]), 0)
        seen = pos <= place
        for h in range(HEADS):
            cols = slice(h * HEAD_DIM, (h + 1) * HEAD_DIM)
            o, total = attend(q_ref[span, cols], kv[:, :HEAD_DIM], kv[:, HEAD_DIM:], seen)
            g = gates[span, HEADS + h : HEADS + h + 1]
            done[span, cols] = (part_ref[span, cols] + o * (g / total)).astype(done.dtype)
        write = pltpu.make_async_copy(done.at[span], out.at[span], out_sem.at[first // WIDE])
        write.start()
        writes.append(write)
    for write in writes:
        write.wait()


def hbm(x):
    return pltpu.with_memory_space_constraint(x, pltpu.MemorySpace.HBM)


def params(mib):
    return pltpu.CompilerParams(vmem_limit_bytes=mib << 20)


def solution(mesh):
    stretches = mesh.shape["blk"]
    group_size = mesh.shape["grp"]
    cores = 2
    ys = group_size // cores
    depth = 8
    up = route(stretches, ys, cores, lambda y, c: (y + 1, c))
    down = route(stretches, ys, cores, lambda y, c: (y - 1, c))
    across = route(stretches, ys, cores, lambda y, c: (y + 2, c))
    swap = route(stretches, ys, cores, lambda y, c: (y, 1 - c))
    behind = [(i * group_size - 1, i * group_size) for i in range(1, stretches)]

    def cross(piece):
        return lax.ppermute(piece, AXES, swap)

    def spread(piece):
        return [lax.ppermute(piece, AXES, path) for path in (up, down, across)]

    def per_device(
        queries, keys, values, selected, key_in, key_out, value_in, value_out, positions, gate_weight
    ):
        ids = jnp.stack([lax.axis_index("blk"), lax.axis_index("grp")]).astype(jnp.int32)
        ids, sel, keys, values, key_in, key_out, value_in, value_out, positions, queries, gate_weight = (
            hbm(x)
            for x in (
                ids,
                selected.T,
                keys,
                values,
                key_in,
                key_out,
                value_in,
                value_out,
                positions,
                queries,
                gate_weight.T,
            )
        )
        toks = queries.shape[0]
        per_dev = toks // SEL_BLOCK
        per_row = group_size * per_dev
        ncomp = toks // CMP_BLOCK
        per_z = stretches // depth * ncomp
        f32_rows = jax.ShapeDtypeStruct(queries.shape, jnp.float32)
        blocks = (SEL_BLOCK, 2 * HEAD_DIM)

        kv, meta = pl.pallas_call(
            prep_kernel,
            in_specs=[SMEM] + [HBM] * 3,
            out_specs=[VMEM] * 2,
            out_shape=[
                jax.ShapeDtypeStruct((toks, 2 * HEAD_DIM), jnp.bfloat16),
                jax.ShapeDtypeStruct((1, stretches * group_size + 128), jnp.int32),
            ],
            scratch_shapes=[
                pltpu.VMEM((2, toks, HEAD_DIM), jnp.bfloat16),
                pltpu.VMEM((TOPN, stretches * group_size), jnp.int32),
                pltpu.SemaphoreType.DMA((3,)),
            ],
            compiler_params=params(8),
            name="prep",
        )(ids, keys, values, sel)
        meta = hbm(meta)
        copies = pl.pallas_call(
            compress_kernel,
            in_specs=[HBM] * 7,
            out_specs=VMEM,
            out_shape=jax.ShapeDtypeStruct((stretches, ncomp, 2 * HEAD_DIM), jnp.bfloat16),
            scratch_shapes=[
                pltpu.VMEM((2, toks, HEAD_DIM), jnp.bfloat16),
                pltpu.VMEM(positions.shape, jnp.bfloat16),
                pltpu.VMEM((2, toks, HEAD_DIM), jnp.float32),
                pltpu.VMEM((2, ncomp, CMP_BLOCK * HEAD_DIM), jnp.bfloat16),
                pltpu.VMEM((2, *key_in.shape), jnp.bfloat16),
                pltpu.VMEM((2, *key_out.shape), jnp.bfloat16),
                pltpu.SemaphoreType.DMA((7,)),
            ],
            compiler_params=params(16),
            name="compress",
        )(keys, values, positions, key_in, key_out, value_in, value_out)
        own = kv.reshape(per_dev, *blocks)
        s_own = cross(own)
        from1, from3, far = spread(own)
        edge = lax.ppermute(own, AXES, behind)
        copies, edge, s_own = lax.optimization_barrier((copies, edge, s_own))
        column_comp = lax.all_to_all(copies, "blk", split_axis=0, concat_axis=0, tiled=True)
        s_from1, s_from3, s_far = cross(from1), cross(from3), cross(far)

        outgoing, nearby = pl.pallas_call(
            pick_kernel,
            in_specs=[SMEM] + [ANY] * 8,
            out_specs=[HBM, HBM],
            out_shape=[
                jax.ShapeDtypeStruct((stretches, *blocks), jnp.bfloat16),
                jax.ShapeDtypeStruct((TOPN, *blocks), jnp.bfloat16),
            ],
            scratch_shapes=[
                pltpu.VMEM((per_row, *blocks), jnp.bfloat16),
                pltpu.SemaphoreType.DMA((stretches + TOPN,)),
            ],
            compiler_params=params(16),
            name="pick",
        )(meta, own, s_own, from1, s_from1, far, s_far, from3, s_from3)
        incoming = lax.all_to_all(outgoing, "blk", split_axis=0, concat_axis=0, tiled=True)

        q_of = pltpu.VMEM(queries.shape, jnp.bfloat16)
        gw_of = pltpu.VMEM(gate_weight.shape, jnp.bfloat16)
        kv_of = pltpu.VMEM((2 * toks, 3 * HEAD_DIM), jnp.bfloat16)
        flat = (toks, 2 * HEAD_DIM)
        local = pl.pallas_call(
            window_kernel,
            in_specs=[SMEM] + [HBM] * 2 + [ANY] * 4,
            out_specs=VMEM,
            out_shape=f32_rows,
            scratch_shapes=[
                q_of,
                gw_of,
                kv_of,
                pltpu.SemaphoreType.DMA((5,)),
            ],
            compiler_params=params(16),
            name="window",
        )(
            meta,
            queries,
            gate_weight,
            kv,
            s_own.reshape(flat),
            s_from1.reshape(flat),
            edge.reshape(flat),
        )

        own_comp = column_comp.reshape(depth, per_z, 2 * HEAD_DIM)
        comp1, comp3, comp_far = spread(own_comp)
        comp1, comp3, local = lax.optimization_barrier((comp1, comp3, local))
        pieces = (own_comp, comp1, comp_far, comp3)

        part = pl.pallas_call(
            coarse_kernel,
            in_specs=[SMEM] + [HBM] * 2 + [ANY] * 9,
            out_specs=VMEM,
            out_shape=f32_rows,
            scratch_shapes=[
                q_of,
                gw_of,
                pltpu.VMEM(queries.shape, jnp.float32),
                pltpu.VMEM((depth, group_size, per_z, 3 * HEAD_DIM), jnp.bfloat16),
                pltpu.VMEM((HEADS, toks, 3 * HEAD_DIM), jnp.float32),
                pltpu.SemaphoreType.DMA((11,)),
            ],
            compiler_params=params(24),
            name="coarse",
        )(meta, queries, gate_weight, local, *(x for piece in pieces for x in (piece, cross(piece))))

        return pl.pallas_call(
            fine_kernel,
            in_specs=[SMEM] + [HBM] * 2 + [VMEM, ANY, ANY],
            out_specs=HBM,
            out_shape=jax.ShapeDtypeStruct(queries.shape, jnp.bfloat16),
            scratch_shapes=[
                q_of,
                gw_of,
                kv_of,
                pltpu.VMEM(queries.shape, jnp.bfloat16),
                pltpu.SemaphoreType.DMA((2,)),
                pltpu.SemaphoreType.DMA((TOPN,)),
                pltpu.SemaphoreType.DMA((toks // WIDE,)),
            ],
            compiler_params=params(20),
            name="fine",
        )(meta, queries, gate_weight, part, nearby, incoming)

    rows = P(AXES, None)
    return jax.shard_map(
        per_device,
        mesh=mesh,
        in_specs=(rows, rows, rows) + (P(),) * 7,
        out_specs=rows,
        check_vma=False,
    )
```
